32 devices in a mesh: dp: 8 (over z, x), mp: 4 (over y, core).
Axes of the slice: x: 2, y: 2, z: 4, core: 2. Of those that a mesh axis runs over, the one named last changes fastest.
Arguments:
- patches: bfloat16 [8192, 1280], P('dp', 'mp'), may hold values from -6 to 6
- cotangent: bfloat16 [8192, 1280], P('dp', 'mp'), may hold values from -0.29882812 to 0.29882812
- encoder_rank: int32 [64], P('dp'), may hold values from 0 to 7, as said below
- block_fill: int32 [64], P('dp'), may hold values from 32 to 128
- w_up: bfloat16 [1280, 5120], P(None, 'mp'), may hold values from -0.15625 to 0.15625
- w_down: bfloat16 [5120, 1280], P('mp'), may hold values from -0.078125 to 0.078125
- q_up: float32 [5120, 64], P('mp'), may hold values from -6 to 6
- q_down: float32 [1280, 64], replicated, may hold values from -6 to 6
Outputs:
- encoded: bfloat16 [14336, 1280], P('dp', 'mp')
- approx_up: float32 [1280, 5120], P(None, 'mp')
- approx_down: float32 [5120, 1280], P('mp')
- qnew_up: float32 [5120, 64], P('mp')
- qnew_down: float32 [1280, 64], replicated
The draws below stay inside these ranges and needn't reach their ends.
Inputs may be any that keep to these rules, and one draw needn't show every extreme that they name: `encoder_rank`: from the blocks of one data rank at most 2 go to one encoder rank, and one encoder rank receives at most 14 blocks in all; both bounds are reached in every draw. Every encoder rank receives some block.
All inputs are finite; a program needn't handle non-finite values.
Results may differ from the reference program's by a relative error of at most 0.015.
Values may be sent and summed in bfloat16 or wider, within the bound.
No kernel may reach another device: no remote copies, remote signals or barrier semaphores. Data moves between devices by JAX's collectives and lax.ppermute only.
A program may use at most 128 MiB of HBM per device.

```python
import jax
import jax.numpy as jnp
from jax import lax

D = 1280
FF = 5120
BLOCK = 128
RANK = 64
BLK_DEV = 8
RMAX = 14
BLOCKS = 64
TOKENS = 8192
N_DP = 8


def draw_encoder_rank(key, part):
    base_key = jax.random.fold_in(key, 7)
    key_order, key_shift, key_column = jax.random.split(base_key, 3)
    ordering = jax.random.permutation(key_order, N_DP).astype(jnp.int32)
    uniform_cols = BLK_DEV - 2
    hot_count = N_DP // 4
    shifts = jax.random.permutation(key_shift, N_DP)[:uniform_cols].astype(jnp.int32)
    sources = jnp.arange(N_DP, dtype=jnp.int32)
    spread = (sources[:, None] + shifts[None, :]) % N_DP
    lead_col = spread[:, 0]
    hot_index = (lead_col[:, None] + jnp.arange(2, dtype=jnp.int32)[None, :]) % hot_count
    dest_table = jnp.concatenate([spread, hot_index], axis=1)
    columns = jax.random.permutation(key_column, BLK_DEV)
    dest_table = dest_table[:, columns]
    return ordering[dest_table].reshape(-1).astype(jnp.int32)


def place_ends(values, own_key, smallest, top_value):
    place = [jax.random.randint(jax.random.fold_in(own_key, axis), (), 0, length) for axis, length in enumerate(values.shape)]
    widest = values.shape.index(max(values.shape))
    next_to = place[:widest] + [(place[widest] + 1) % values.shape[widest]] + place[widest + 1:]
    return values.at[tuple(place)].set(smallest).at[tuple(next_to)].set(top_value)


def levels(own_key, dims, cuts, low, top_value):
    def one(dim, blocks):
        steps = jax.random.uniform(jax.random.fold_in(jax.random.fold_in(own_key, 6), dim), (blocks,), jnp.float32, low / len(cuts), top_value / len(cuts))
        return jnp.repeat(jnp.exp(steps), dims[dim] // blocks).reshape((-1,) + (1,) * (len(dims) - dim - 1))

    loudness = one(*cuts[0])
    for cut in cuts[1:]:
        loudness = loudness * one(*cut)
    return loudness


def gaussian(stream_key, extent, deviation, most, shards=(), held_as=jnp.bfloat16):
    gain = levels(stream_key, extent, shards, -0.22, 0.18) if shards else 1.0
    entries = jax.random.normal(stream_key, extent, jnp.float32) * deviation * gain
    return jnp.minimum(jnp.maximum(entries, -most), most).astype(held_as)


def setup_inputs(seed: int = 0) -> dict:
    keys = jax.random.split(jax.random.key(seed), 9)
    patches = gaussian(keys[0], (TOKENS, D), 1.0, 6.0, ((0, 8), (1, 4)))
    cotangent = gaussian(keys[1], (TOKENS, D), 0.05, 0.29882812, ((0, 8), (1, 4)))
    encoder_rank = draw_encoder_rank(jax.random.fold_in(keys[8], 71), 0)
    block_fill = place_ends(jax.random.randint(keys[3], (BLOCKS,), BLOCK // 4, BLOCK + 1), jax.random.fold_in(keys[3], 1), BLOCK // 4, BLOCK).astype(jnp.int32)
    w_up = gaussian(keys[4], (D, FF), D ** -0.5, 0.15625, ((1, 4),))
    w_down = gaussian(keys[5], (FF, D), FF ** -0.5, 0.078125, ((0, 4),))
    q_up = gaussian(keys[6], (FF, RANK), 1.0, 6.0, ((0, 4),), jnp.float32)
    q_down = gaussian(keys[7], (D, RANK), 1.0, 6.0, (), jnp.float32)
    return dict(patches=patches, cotangent=cotangent, encoder_rank=encoder_rank, block_fill=block_fill, w_up=w_up, w_down=w_down, q_up=q_up, q_down=q_down)


def gelu_parts(preact):
    sig = jax.nn.sigmoid(1.702 * preact)
    return (preact * sig, sig + 1.702 * preact * sig * (1.0 - sig))

def compress(grad, warm):
    highest = lax.Precision.HIGHEST
    proj = jnp.dot(grad, warm, precision=highest)
    gram = jnp.dot(proj.T, proj, precision=highest)
    lower = jnp.linalg.cholesky(gram)
    basis = jax.scipy.linalg.solve_triangular(lower, proj.T, lower=True).T
    fresh = jnp.dot(grad.T, basis, precision=highest)
    return (fresh, jnp.dot(basis, fresh.T, precision=highest))

def reference(patches, cotangent, encoder_rank, block_fill, w_up, w_down, q_up, q_down):
    total_rows = patches.shape[0]
    row_ids = jnp.arange(total_rows, dtype=jnp.int32)
    within = row_ids % BLOCK
    owner = row_ids // BLOCK
    keep = (within < block_fill[owner])[:, None]
    preact = jnp.dot(patches.astype(jnp.float32), w_up.astype(jnp.float32), preferred_element_type=jnp.float32)
    active, slope = gelu_parts(preact)
    hidden = active.astype(jnp.bfloat16)
    out_rows = jnp.where(keep, jnp.dot(hidden.astype(jnp.float32), w_down.astype(jnp.float32), preferred_element_type=jnp.float32), 0.0).astype(jnp.bfloat16)
    masked_cot = jnp.where(keep, cotangent, jnp.zeros((), jnp.bfloat16))
    grad_hidden = lax.dot_general(masked_cot.astype(jnp.float32), w_down.astype(jnp.float32), (((1,), (1,)), ((), ())), preferred_element_type=jnp.float32)
    grad_pre = (grad_hidden * slope).astype(jnp.bfloat16)
    grad_up = lax.dot_general(patches.astype(jnp.float32), grad_pre.astype(jnp.float32), (((0,), (0,)), ((), ())), preferred_element_type=jnp.float32)
    grad_down = lax.dot_general(hidden.astype(jnp.float32), masked_cot.astype(jnp.float32), (((0,), (0,)), ((), ())), preferred_element_type=jnp.float32)
    block_ids = jnp.arange(BLOCKS, dtype=jnp.int32)
    before = (encoder_rank[None, :] == encoder_rank[:, None]) & (block_ids[None, :] < block_ids[:, None])
    ordinal = jnp.sum(before.astype(jnp.int32), axis=1).astype(jnp.int32)
    target = (encoder_rank * RMAX + ordinal).astype(jnp.int32)
    placed = jnp.zeros((N_DP * RMAX, BLOCK, D), jnp.bfloat16)
    placed = placed.at[target].set(out_rows.reshape(BLOCKS, BLOCK, D))
    encoded = placed.reshape(N_DP * RMAX * BLOCK, D)
    qnew_up, approx_up = compress(grad_up, q_up)
    qnew_down, approx_down = compress(grad_down, q_down)
    return (encoded, approx_up, approx_down, qnew_up, qnew_down)
```

```python
import functools

import jax
import jax.numpy as jnp
from jax import lax
from jax.experimental import pallas as pl
from jax.experimental.pallas import tpu as pltpu
from jax.sharding import PartitionSpec as P

BLOCK = 128
CAP = 2
EXTRA = 6
bf16 = jnp.bfloat16
f32 = jnp.float32


def bits_of(count):
    return [1 << b for b in range(count.bit_length() - 1)]


def swap(x, axis, bit):
    count = lax.axis_size(axis)
    return lax.ppermute(x, axis, [(i, i ^ bit) for i in range(count)])


def gather_xor(own):
    count = lax.axis_size("mp")
    even = {0: own}
    for bit in bits_of(count)[1:]:
        even.update({o | bit: swap(p, "mp", bit) for o, p in even.items()})
    pieces = dict(even)
    pieces.update({o | 1: swap(p, "mp", 1) for o, p in even.items()})
    return [pieces[o] for o in range(count)]


def reorder(pieces, me):
    for bit in bits_of(len(pieces)):
        flip = (me & bit) != 0
        pieces = [jnp.where(flip, pieces[i ^ bit], pieces[i]) for i in range(len(pieces))]
    return pieces


def slices(x, count, axis):
    size = x.shape[axis] // count
    return [lax.slice_in_dim(x, i * size, (i + 1) * size, axis=axis) for i in range(count)]


def reduce_mp(pieces, send_type):
    pieces = dict(enumerate(pieces))
    for bit in bits_of(len(pieces)):
        out = [o for o in pieces if o & bit]
        sent = swap(jnp.concatenate([pieces[o].astype(send_type) for o in out], axis=1), "mp", bit)
        got = slices(sent, len(out), 1)
        pieces = {o ^ bit: pieces[o ^ bit] + g.astype(f32) for o, g in zip(out, got)}
    return pieces[0]


def spread_mp(own):
    have = own
    offsets = [0]
    for bit in reversed(bits_of(lax.axis_size("mp"))):
        got = swap(have, "mp", bit)
        have = jnp.concatenate([have, got], axis=1)
        offsets = offsets + [o | bit for o in offsets]
    parts = slices(have, len(offsets), 1)
    return [parts[offsets.index(o)] for o in range(len(offsets))]


def sum_over(x, axis, send_type):
    for bit in bits_of(lax.axis_size(axis)):
        mine = x.astype(send_type)
        x = mine.astype(f32) + swap(mine, axis, bit).astype(f32)
    return x


def halves(x, axis):
    head = lax.reduce_precision(x, 8, 7)
    tail = (x - head).astype(bf16)
    return jnp.concatenate([head.astype(bf16), tail], axis=axis)


def fold(x, axis):
    a, b = slices(x, 2, axis)
    return a + b


def dot(a, b, dims):
    return lax.dot_general(a, b, ((dims[:1], dims[1:]), ((), ())), preferred_element_type=f32)


def pick_kernel(index_ref, ok_ref, in_ref, out_ref):
    ok = ok_ref[pl.program_id(0)] > 0
    out_ref[...] = jnp.where(ok, in_ref[...], jnp.zeros_like(in_ref))


def pick_blocks(blocks, index, ok):
    width = blocks.shape[1]
    return pl.pallas_call(
        pick_kernel,
        out_shape=jax.ShapeDtypeStruct((index.shape[0] * BLOCK, width), blocks.dtype),
        grid_spec=pltpu.PrefetchScalarGridSpec(
            num_scalar_prefetch=2,
            grid=(index.shape[0],),
            in_specs=[pl.BlockSpec((BLOCK, width), lambda k, index, ok: (index[k], 0))],
            out_specs=pl.BlockSpec((BLOCK, width), lambda k, index, ok: (k, 0)),
        ),
        cost_estimate=pl.CostEstimate(
            flops=0, transcendentals=0, bytes_accessed=4 * index.shape[0] * BLOCK * width
        ),
    )(index, ok, blocks)


def earlier(labels):
    ids = jnp.arange(labels.shape[0], dtype=jnp.int32)
    same = (labels[:, None] == labels[None, :]) & (ids[None, :] < ids[:, None])
    return jnp.sum(same.astype(jnp.int32), axis=1)


def send_plan(ranks, ranks_dp):
    place = ranks * CAP + earlier(ranks)
    chosen = jnp.arange(ranks_dp * CAP, dtype=jnp.int32)[:, None] == place[None, :]
    ids = jnp.arange(ranks.shape[0], dtype=jnp.int32)
    index = jnp.sum(jnp.where(chosen, ids[None, :], 0), axis=1)
    return index.astype(jnp.int32), jnp.any(chosen, axis=1).astype(jnp.int32)


def recv_plan(all_ranks, per_rank, me, most):
    total = all_ranks.shape[0]
    ids = jnp.arange(total, dtype=jnp.int32)
    source = ids // per_rank
    order = earlier(all_ranks)
    within = earlier(all_ranks + source * total)
    place = source * CAP + within
    mine = all_ranks == me
    chosen = mine[None, :] & (order[None, :] == jnp.arange(most, dtype=jnp.int32)[:, None])
    index = jnp.sum(jnp.where(chosen, place[None, :], 0), axis=1)
    return index.astype(jnp.int32), jnp.any(chosen, axis=1).astype(jnp.int32)


def all_ranks_of(ranks, me):
    count = lax.axis_size("dp")
    table = jnp.where(jnp.arange(count, dtype=jnp.int32)[:, None] == me, ranks[None, :], 0)
    for bit in bits_of(count):
        table = table + swap(table, "dp", bit)
    return table.reshape(-1)


def inverse_factor(gram):
    lower = jnp.linalg.cholesky(gram)
    return jax.scipy.linalg.solve_triangular(lower, jnp.eye(gram.shape[0], dtype=f32), lower=True)


def local(patches, cotangent, encoder_rank, block_fill, w_up, w_down, q_up, q_down):
    ranks_dp = lax.axis_size("dp")
    count = lax.axis_size("mp")
    me, me_dp = lax.axis_index("mp"), lax.axis_index("dp")
    blocks = encoder_rank.shape[0]
    features = patches.shape[1]
    high = lax.Precision.HIGHEST

    x = jnp.concatenate(gather_xor(patches), axis=1)
    c = jnp.concatenate(gather_xor(cotangent), axis=1)
    every = all_ranks_of(encoder_rank, me_dp)
    w1 = jnp.concatenate(reorder(slices(w_up, count, 0), me), axis=0)
    w2 = jnp.concatenate(reorder(slices(w_down, count, 1), me), axis=1)
    qd = halves(jnp.concatenate(reorder(slices(q_down, count, 0), me), axis=0), 1)
    qu = halves(q_up, 1)

    within = jnp.arange(BLOCK, dtype=jnp.int32)
    keep = (within[None, :] < block_fill[:, None]).reshape(-1, 1)

    preact = dot(x, w1, (1, 0))
    sig = jax.nn.sigmoid(1.702 * preact)
    hidden = (preact * sig).astype(bf16)
    slope = sig + 1.702 * preact * sig * (1.0 - sig)
    partial = jnp.where(keep, dot(hidden, w2, (1, 0)), 0.0)

    c = jnp.where(keep, c, jnp.zeros((), bf16))
    grad_pre = (dot(c, w2, (1, 1)) * slope).astype(bf16)
    u = fold(dot(grad_pre, qu, (1, 0)), 1)
    t = fold(dot(c, qd, (1, 0)), 1)
    proj_up = fold(dot(halves(u, 1), x, (0, 0)), 0)
    proj_down = fold(dot(halves(t, 1), hidden, (0, 0)), 0)

    proj_down = sum_over(proj_down, "dp", bf16)
    proj_up = sum_over(reduce_mp(slices(proj_up, count, 1), f32), "dp", f32)
    proj_up = jnp.concatenate(spread_mp(proj_up), axis=1)

    v2 = fold(dot(hidden, halves(proj_down, 0), (1, 1)), 1)
    raw_down = fold(dot(halves(v2, 1), c, (0, 0)), 0)
    v = fold(dot(x, halves(proj_up, 0), (1, 1)), 1)
    raw_up = fold(dot(halves(v, 1), grad_pre, (0, 0)), 0)

    gram_up = jnp.dot(proj_up, proj_up.T, precision=high)
    gram_down = sum_over(jnp.dot(proj_down, proj_down.T, precision=high), "mp", f32)
    inv_up = inverse_factor(gram_up)
    inv_down = inverse_factor(gram_down)
    basis_up = jnp.dot(inv_up, proj_up, precision=high)
    basis_up = jnp.concatenate(reorder(slices(basis_up, count, 1), me), axis=1)
    basis_down = jnp.dot(inv_down, proj_down, precision=high)

    raw_up = sum_over(raw_up, "dp", bf16)
    raw_down = sum_over(reduce_mp(slices(raw_down, count, 1), f32), "dp", f32)
    raw_down = jnp.concatenate(reorder(spread_mp(raw_down), me), axis=1)
    fresh_up = jnp.dot(inv_up, raw_up, precision=high)
    fresh_down = jnp.dot(inv_down, raw_down, precision=high)
    approx_up = lax.dot_general(basis_up, fresh_up, (((0,), (0,)), ((), ())), precision=lax.Precision.HIGH)
    approx_down = lax.dot_general(basis_down, fresh_down, (((0,), (0,)), ((), ())), precision=lax.Precision.HIGH)

    own = reduce_mp(slices(partial, count, 1), bf16).astype(bf16)
    sent = pick_blocks(own, *send_plan(encoder_rank, ranks_dp))
    got = lax.all_to_all(sent, "dp", split_axis=0, concat_axis=0, tiled=True)
    encoded = pick_blocks(got, *recv_plan(every, blocks, me_dp, blocks + EXTRA))
    return (encoded, approx_up, approx_down, fresh_up.T, fresh_down.T)


def solution(mesh):
    placed = (
        P("dp", "mp"),
        P("dp", "mp"),
        P("dp"),
        P("dp"),
        P(None, "mp"),
        P("mp", None),
        P("mp", None),
        P(),
    )
    return jax.shard_map(
        local,
        mesh=mesh,
        in_specs=placed,
        out_specs=(P("dp", "mp"), P(None, "mp"), P("mp", None), P("mp", None), P()),
        check_vma=False,
    )
```

```python
import functools

import jax
import jax.numpy as jnp
from jax import lax
from jax.experimental import pallas as pl
from jax.experimental.pallas import tpu as pltpu
from jax.sharding import PartitionSpec as P

BLOCK = 128
TILE = 256
CAP = 2
EXTRA = 6
bf16 = jnp.bfloat16
f32 = jnp.float32
HIGHEST = lax.Precision.HIGHEST


def bits_of(count):
    return [1 << b for b in range(count.bit_length() - 1)]


def swap(x, axis, bit):
    count = lax.axis_size(axis)
    return lax.ppermute(x, axis, [(i, i ^ bit) for i in range(count)])


def gather_xor(own):
    count = lax.axis_size("mp")
    pieces = {0: own}
    for bit in bits_of(count)[1:]:
        pieces.update({o | bit: swap(p, "mp", bit) for o, p in list(pieces.items())})
    pieces.update({o | 1: swap(p, "mp", 1) for o, p in list(pieces.items())})
    return [pieces[o] for o in range(count)]


def reorder(pieces, me):
    for bit in bits_of(len(pieces)):
        flip = (me & bit) != 0
        pieces = [jnp.where(flip, pieces[i ^ bit], pieces[i]) for i in range(len(pieces))]
    return pieces


def slices(x, count, axis):
    size = x.shape[axis] // count
    return [lax.slice_in_dim(x, i * size, (i + 1) * size, axis=axis) for i in range(count)]


def reduce_mp(even, odd):
    have = even + swap(odd, "mp", 1)
    for bit in bits_of(lax.axis_size("mp"))[1:]:
        have = have.reshape(have.shape[0] // 2, 2, *have.shape[1:])
        have = have[:, 0] + swap(have[:, 1], "mp", bit)
    return have[0]


def spread_mp(own):
    have = {0: own}
    for bit in reversed(bits_of(lax.axis_size("mp"))):
        offsets = sorted(have)
        if len(offsets) == 1:
            got = [swap(have[0], "mp", bit)]
        else:
            sent = swap(jnp.stack([have[o] for o in offsets]), "mp", bit)
            got = [sent[i] for i in range(len(offsets))]
        have.update({o | bit: g for o, g in zip(offsets, got)})
    return [have[o] for o in range(len(have))]


def sum_over(x, axis, send_type):
    for bit in bits_of(lax.axis_size(axis)):
        mine = x.astype(send_type)
        x = mine.astype(f32) + swap(mine, axis, bit).astype(f32)
    return x


def dot(a, b, contract=(1, 0), precision=None):
    dims = (((contract[0],), (contract[1],)), ((), ()))
    return lax.dot_general(a, b, dims, preferred_element_type=f32, precision=precision)


def head_tail(x):
    head = x.astype(bf16)
    return head, (x - head.astype(f32)).astype(bf16)


def stacked(x):
    return jnp.concatenate(head_tail(x), axis=0)


def fold(x):
    rows = x.shape[0] // 2
    return x[:rows] + x[rows:]


def call(body, out_shape, args, scalars=(), grid=(1,), in_specs=None, out_specs=None, scratch=(), flops=0):
    moved = sum(a.size * a.dtype.itemsize for a in args)
    moved += sum(o.size * o.dtype.itemsize for o in jax.tree.leaves(out_shape))
    return pl.pallas_call(
        body,
        out_shape=out_shape,
        grid_spec=pltpu.PrefetchScalarGridSpec(
            num_scalar_prefetch=len(scalars),
            grid=grid,
            in_specs=in_specs,
            out_specs=out_specs,
            scratch_shapes=list(scratch),
        ),
        cost_estimate=pl.CostEstimate(flops=flops, transcendentals=0, bytes_accessed=moved),
        compiler_params=pltpu.CompilerParams(vmem_limit_bytes=48 << 20),
    )(*scalars, *args)


def whole(x):
    return pl.BlockSpec(x.shape, lambda *_: (0,) * len(x.shape), pipeline_mode=pl.Buffered(1))


def tokens_of(x):
    return pl.BlockSpec((x.shape[0], TILE), lambda i, *_: (0, i))


def struct(shape, dtype):
    return jax.ShapeDtypeStruct(shape, dtype)


def prepare_kernel(count, me_ref, up_ref, down_ref, up_t_ref, down_t_ref, down_x_ref, held):
    me = me_ref[0]
    features, hidden = up_ref.shape
    piece = features // count
    strip = TILE
    for o in range(count):
        rows = pl.ds(pl.multiple_of((me ^ o) * piece, piece), piece)
        held[o * piece : (o + 1) * piece, :] = up_ref[rows, :]

    for k in range(0, hidden, strip):
        up_t_ref[k : k + strip, :] = held[:, k : k + strip].T
    for k in range(0, down_ref.shape[0], strip):
        held[:, k : k + strip] = down_ref[k : k + strip, :].T
    for o in range(count):
        rows = pl.ds(pl.multiple_of((me ^ o) * piece, piece), piece)
        down_t_ref[o * piece : (o + 1) * piece, :] = held[rows, :]
    for k in range(0, down_ref.shape[0], strip):
        down_x_ref[k : k + strip, :] = down_t_ref[:, k : k + strip].T


def prepare(w_up, w_down, me, count):
    features, hidden = w_up.shape
    outs = (struct((hidden, features), bf16), struct((features, hidden), bf16), struct((hidden, features), bf16))
    return call(
        functools.partial(prepare_kernel, count),
        outs,
        (w_up, w_down),
        (me.reshape(1),),
        in_specs=[whole(w_up), whole(w_down)],
        out_specs=[whole(o) for o in outs],
        scratch=[pltpu.VMEM((features, hidden), bf16)],
    )


def assemble(refs, held):
    at = 0
    for ref in refs:
        held[at : at + ref.shape[0], :] = ref[...]
        at += ref.shape[0]


def lanes_kept(fill_ref, block):
    return lax.broadcasted_iota(jnp.int32, (1, BLOCK), 1) < fill_ref[block]


def mask_tokens(x, fill_ref):
    per = TILE // BLOCK
    parts = []
    for b in range(per):
        keep = lanes_kept(fill_ref, pl.program_id(0) * per + b)
        part = x[:, b * BLOCK : (b + 1) * BLOCK]
        parts.append(jnp.where(keep, part, jnp.zeros_like(part)))
    return jnp.concatenate(parts, axis=1)


def forward_kernel(count, fill_ref, *refs):
    x_refs, (up_t_ref, down_t_ref), refs = refs[:count], refs[count : count + 2], refs[count + 2 :]
    hidden_ref, slope_ref, out_refs, held = refs[0], refs[1], refs[2:-1], refs[-1]
    assemble(x_refs, held)
    preact = dot(up_t_ref[...], held[...])
    sig = jax.nn.sigmoid(1.702 * preact)
    active = preact * sig
    hidden_ref[...] = active.astype(bf16)
    slope_ref[...] = (sig + 1.702 * active * (1.0 - sig)).astype(bf16)
    out = mask_tokens(dot(down_t_ref[...], hidden_ref[...]), fill_ref).astype(bf16)
    piece = out.shape[0] // count
    for o, ref in enumerate(out_refs):
        ref[...] = out[o * piece : (o + 1) * piece]


def forward(xs, up_t, down_t, fill):
    count = len(xs)
    piece, total = xs[0].shape
    hidden, features = up_t.shape
    outs = [struct((hidden, total), bf16)] * 2 + [struct((piece, total), bf16)] * count
    got = call(
        functools.partial(forward_kernel, count),
        outs,
        (*xs, up_t, down_t),
        (fill,),
        grid=(total // TILE,),
        in_specs=[tokens_of(x) for x in xs] + [whole(up_t), whole(down_t)],
        out_specs=[tokens_of(o) for o in outs],
        scratch=[pltpu.VMEM((features, TILE), bf16)],
        flops=4 * features * hidden * total,
    )
    return got[0], got[1], got[2:]


def write_pieces(value, even_ref, odd_ref):
    half, _, piece = even_ref.shape
    for o in range(2 * half):
        part = value[:, o * piece : (o + 1) * piece]
        (odd_ref if o & 1 else even_ref)[o // 2] = part


def backward_kernel(count, fill_ref, *refs):
    c_refs, x_refs, refs = refs[:count], refs[count : 2 * count], refs[2 * count :]
    slope_ref, hidden_ref, down_x_ref, qu_ref, qd_ref = refs[:5]
    grad_ref, even_ref, odd_ref, down_ref, held_c, held_x, acc_up, acc_down = refs[5:]
    step = pl.program_id(0)

    @pl.when(step == 0)
    def _():
        acc_up[...] = jnp.zeros_like(acc_up)
        acc_down[...] = jnp.zeros_like(acc_down)

    assemble(c_refs, held_c)
    assemble(x_refs, held_x)
    held_c[...] = mask_tokens(held_c[...], fill_ref)
    grad = dot(down_x_ref[...], held_c[...])
    grad_ref[...] = (grad * slope_ref[...].astype(f32)).astype(bf16)
    t = fold(dot(qd_ref[...], held_c[...]))
    acc_down[...] += fold(dot(stacked(t), hidden_ref[...], (1, 1)))
    u = fold(dot(qu_ref[...], grad_ref[...]))
    acc_up[...] += fold(dot(stacked(u), held_x[...], (1, 1)))

    @pl.when(step == pl.num_programs(0) - 1)
    def _():
        down_ref[...] = acc_down[...]
        write_pieces(acc_up[...], even_ref, odd_ref)


def backward(cs, xs, slope, hidden, down_x, qu, qd, fill):
    count = len(xs)
    piece, total = xs[0].shape
    units, features = down_x.shape
    rank = qu.shape[0] // 2
    pieces = struct((count // 2, rank, piece), f32)
    outs = [struct((units, total), bf16), pieces, pieces, struct((rank, units), f32)]
    return call(
        functools.partial(backward_kernel, count),
        outs,
        (*cs, *xs, slope, hidden, down_x, qu, qd),
        (fill,),
        grid=(total // TILE,),
        in_specs=[tokens_of(x) for x in (*cs, *xs, slope, hidden)] + [whole(x) for x in (down_x, qu, qd)],
        out_specs=[tokens_of(outs[0])] + [whole(o) for o in outs[1:]],
        scratch=[
            pltpu.VMEM((features, TILE), bf16),
            pltpu.VMEM((features, TILE), bf16),
            pltpu.VMEM((rank, features), f32),
            pltpu.VMEM((rank, units), f32),
        ],
        flops=2 * features * units * total,
    )


def two_sided_kernel(n_left, n_first, n_second, masked, fill_ref, *refs):
    left_refs, refs = refs[:n_left], refs[n_left:]
    first_refs, refs = refs[:n_first], refs[n_first:]
    second_refs, refs = refs[:n_second], refs[n_second:]
    out_refs, (left, first, second, acc) = refs[:-4], refs[-4:]
    rank = left_refs[0].shape[0]

    @pl.when(pl.program_id(0) == 0)
    def _():
        acc[...] = jnp.zeros_like(acc)
        joined = jnp.concatenate([r[...] for r in left_refs], axis=1)
        left[...] = stacked(joined)

    assemble(first_refs, first)
    assemble(second_refs, second)
    v = fold(dot(left[...], first[...]))
    if masked:
        v = mask_tokens(v, fill_ref)
    acc[...] += fold(dot(stacked(v), second[...], (1, 1)))

    @pl.when(pl.program_id(0) == pl.num_programs(0) - 1)
    def _():
        if masked:
            write_pieces(acc[...], *out_refs)
        else:
            out_refs[0][...] = acc[...]


def two_sided(lefts, firsts, seconds, fill, masked):
    rank = lefts[0].shape[0]
    total = firsts[0].shape[1]
    inner = sum(x.shape[0] for x in firsts)
    outer = sum(x.shape[0] for x in seconds)
    if masked:
        pieces = struct((len(seconds) // 2, rank, seconds[0].shape[0]), f32)
        outs = [pieces, pieces]
    else:
        outs = [struct((rank, outer), f32)]
    return call(
        functools.partial(two_sided_kernel, len(lefts), len(firsts), len(seconds), masked),
        outs,
        (*lefts, *firsts, *seconds),
        (fill,),
        grid=(total // TILE,),
        in_specs=[whole(x) for x in lefts] + [tokens_of(x) for x in (*firsts, *seconds)],
        out_specs=[whole(o) for o in outs],
        scratch=[
            pltpu.VMEM((2 * rank, inner), bf16),
            pltpu.VMEM((inner, TILE), bf16),
            pltpu.VMEM((outer, TILE), bf16),
            pltpu.VMEM((rank, outer), f32),
        ],
        flops=4 * rank * (inner + outer) * total,
    )


def outer_kernel(n_raw, me_ref, inv_ref, basis_ref, *refs):
    raw_refs, (fresh_ref, approx_ref, right) = refs[:n_raw], refs[n_raw:]

    @pl.when(pl.program_id(0) == 0)
    def _():
        raw = jnp.concatenate(reorder([r[...] for r in raw_refs], me_ref[0]), axis=1)
        fresh = dot(inv_ref[...], raw, precision=HIGHEST)
        fresh_ref[...] = fresh
        head, tail = head_tail(fresh)
        right[...] = jnp.concatenate([head, tail, head], axis=0)

    head, tail = head_tail(basis_ref[...])
    approx_ref[...] = dot(jnp.concatenate([head, head, tail], axis=0), right[...], (0, 0))


def outer(inv, basis, raws, me):
    rank, rows = basis.shape
    columns = sum(r.shape[1] for r in raws)
    outs = [struct((rank, columns), f32), struct((rows, columns), f32)]
    return call(
        functools.partial(outer_kernel, len(raws)),
        outs,
        (inv, basis, *raws),
        (me.reshape(1),),
        grid=(rows // BLOCK // 2 if rows % (2 * BLOCK) == 0 else rows // BLOCK,),
        in_specs=[whole(inv), pl.BlockSpec((rank, 2 * BLOCK if rows % (2 * BLOCK) == 0 else BLOCK), lambda i, *_: (0, i))]
        + [whole(r) for r in raws],
        out_specs=[
            whole(outs[0]),
            pl.BlockSpec((2 * BLOCK if rows % (2 * BLOCK) == 0 else BLOCK, columns), lambda i, *_: (i, 0)),
        ],
        scratch=[pltpu.VMEM((3 * rank, columns), bf16)],
        flops=6 * rank * rows * columns,
    )


def pack_kernel(index_ref, a_ref, b_ref, out_ref):
    for s in range(out_ref.shape[0]):
        lanes = pl.ds(pl.multiple_of(index_ref[s] * BLOCK, BLOCK), BLOCK)
        total = a_ref[:, lanes].astype(f32) + b_ref[:, lanes].astype(f32)
        out_ref[s] = total.astype(bf16)


def pack(a, b, index):
    out = struct((index.shape[0], a.shape[0], BLOCK), bf16)
    return call(pack_kernel, out, (a, b), (index,), in_specs=[whole(a), whole(b)], out_specs=whole(out))


def unpack_kernel(index_ref, ok_ref, in_ref, out_ref):
    for k in range(out_ref.shape[1] // BLOCK):
        part = in_ref[index_ref[k]]
        out_ref[:, k * BLOCK : (k + 1) * BLOCK] = jnp.where(ok_ref[k] > 0, part, jnp.zeros_like(part))


def unpack(got, index, ok):
    out = struct((got.shape[1], index.shape[0] * BLOCK), bf16)
    return call(unpack_kernel, out, (got,), (index, ok), in_specs=[whole(got)], out_specs=whole(out))


def earlier(labels):
    ids = jnp.arange(labels.shape[0], dtype=jnp.int32)
    same = (labels[:, None] == labels[None, :]) & (ids[None, :] < ids[:, None])
    return jnp.sum(same.astype(jnp.int32), axis=1)


def send_plan(ranks, ranks_dp):
    place = ranks * CAP + earlier(ranks)
    chosen = jnp.arange(ranks_dp * CAP, dtype=jnp.int32)[:, None] == place[None, :]
    ids = jnp.arange(ranks.shape[0], dtype=jnp.int32)
    return jnp.sum(jnp.where(chosen, ids[None, :], 0), axis=1).astype(jnp.int32)


def recv_plan(all_ranks, per_rank, me, most):
    total = all_ranks.shape[0]
    ids = jnp.arange(total, dtype=jnp.int32)
    source = ids // per_rank
    order = earlier(all_ranks)
    within = earlier(all_ranks + source * total)
    place = source * CAP + within
    mine = all_ranks == me
    chosen = mine[None, :] & (order[None, :] == jnp.arange(most, dtype=jnp.int32)[:, None])
    index = jnp.sum(jnp.where(chosen, place[None, :], 0), axis=1)
    return index.astype(jnp.int32), jnp.any(chosen, axis=1).astype(jnp.int32)


def all_ranks_of(ranks, me):
    count = lax.axis_size("dp")
    table = jnp.where(jnp.arange(count, dtype=jnp.int32)[:, None] == me, ranks[None, :], 0)
    for bit in bits_of(count):
        table = table + swap(table, "dp", bit)
    return table.reshape(-1)


def inverse_factor(gram):
    lower = jnp.linalg.cholesky(gram)
    return jax.scipy.linalg.solve_triangular(lower, jnp.eye(gram.shape[0], dtype=f32), lower=True)


def split_rows(x):
    head = lax.reduce_precision(x, 8, 7)
    return jnp.concatenate([head.astype(bf16), (x - head).astype(bf16)], axis=0)


def local(patches, cotangent, encoder_rank, block_fill, w_up, w_down, q_up, q_down):
    ranks_dp = lax.axis_size("dp")
    count = lax.axis_size("mp")
    me, me_dp = lax.axis_index("mp"), lax.axis_index("dp")
    blocks = encoder_rank.shape[0]

    xs = gather_xor(patches.T)
    cs = gather_xor(cotangent.T)
    every = all_ranks_of(encoder_rank, me_dp)
    up_t, down_t, down_x = prepare(w_up, w_down, me, count)
    qd = split_rows(jnp.concatenate(reorder(slices(q_down.T, count, 1), me), axis=1))
    qu = split_rows(q_up.T)

    hidden, slope, outs = forward(xs, up_t, down_t, block_fill)
    grad_pre, even, odd, proj_down = backward(cs, xs, slope, hidden, down_x, qu, qd, block_fill)

    proj_down = sum_over(proj_down, "dp", bf16)
    proj_up = spread_mp(sum_over(reduce_mp(even, odd), "dp", f32))

    even, odd = two_sided([proj_down], [hidden], cs, block_fill, True)
    (raw_up,) = two_sided(proj_up, xs, [grad_pre], block_fill, False)
    proj_up = jnp.concatenate(reorder(proj_up, me), axis=1)

    gram_up = jnp.dot(proj_up, proj_up.T, precision=HIGHEST)
    gram_down = sum_over(jnp.dot(proj_down, proj_down.T, precision=HIGHEST), "mp", f32)
    inv_up = inverse_factor(gram_up)
    inv_down = inverse_factor(gram_down)
    basis_up = jnp.dot(inv_up, proj_up, precision=HIGHEST)
    basis_down = jnp.dot(inv_down, proj_down, precision=HIGHEST)

    raw_up = sum_over(raw_up, "dp", bf16)
    raw_down = spread_mp(sum_over(reduce_mp(even, odd), "dp", f32))
    fresh_up, approx_up = outer(inv_up, basis_up, [raw_up], me)
    fresh_down, approx_down = outer(inv_down, basis_down, raw_down, me)

    have = dict(enumerate(outs))
    have = {o - 1: (have[o - 1].astype(f32) + swap(have[o], "mp", 1).astype(f32)).astype(bf16) for o in have if o & 1}
    for bit in bits_of(count)[1:]:
        got = {o ^ bit: swap(have[o], "mp", bit) for o in have if o & bit}
        if len(got) == 1:
            break
        have = {o: (have[o].astype(f32) + got[o].astype(f32)).astype(bf16) for o in got}
    sent = pack(have[0], got[0], send_plan(encoder_rank, ranks_dp))
    received = lax.all_to_all(sent, "dp", split_axis=0, concat_axis=0, tiled=True)
    encoded = unpack(received, *recv_plan(every, blocks, me_dp, blocks + EXTRA))
    return (encoded.T, approx_up, approx_down, fresh_up.T, fresh_down.T)


def solution(mesh):
    placed = (
        P("dp", "mp"),
        P("dp", "mp"),
        P("dp"),
        P("dp"),
        P(None, "mp"),
        P("mp", None),
        P("mp", None),
        P(),
    )
    return jax.shard_map(
        local,
        mesh=mesh,
        in_specs=placed,
        out_specs=(P("dp", "mp"), P(None, "mp"), P("mp", None), P("mp", None), P()),
        check_vma=False,
    )
```

```python
import functools

import jax
import jax.numpy as jnp
from jax import lax
from jax.experimental import pallas as pl
from jax.experimental.pallas import tpu as pltpu
from jax.sharding import PartitionSpec as P


BLOCK = 128
TILE = 512
STRIP = 128
CAP = 2
EXTRA = 6
bf16 = jnp.bfloat16
f32 = jnp.float32
HIGHEST = lax.Precision.HIGHEST


def bits_of(count):
    return [1 << b for b in range(count.bit_length() - 1)]


def swap(x, axis, bit):
    count = lax.axis_size(axis)
    return lax.ppermute(x, axis, [(i, i ^ bit) for i in range(count)])


def gather_xor(own):
    count = lax.axis_size("mp")
    pieces = {0: own}
    for bit in bits_of(count)[1:]:
        pieces.update({o | bit: swap(p, "mp", bit) for o, p in list(pieces.items())})
    near = {o | 1: swap(p, "mp", 1) for o, p in pieces.items()}
    pieces.update(near)
    return [pieces[o] for o in range(count)]


def reorder(pieces, me):
    for bit in bits_of(len(pieces)):
        flip = (me & bit) != 0
        pieces = [jnp.where(flip, pieces[i ^ bit], pieces[i]) for i in range(len(pieces))]
    return pieces


def slices(x, count, axis):
    size = x.shape[axis] // count
    return [lax.slice_in_dim(x, i * size, (i + 1) * size, axis=axis) for i in range(count)]


def reduce_mp(even, odd):
    have = even + swap(odd, "mp", 1)
    for bit in bits_of(lax.axis_size("mp"))[1:]:
        have = have.reshape(have.shape[0] // 2, 2, *have.shape[1:])
        have = have[:, 0] + swap(have[:, 1], "mp", bit)
    return have[0]


def spread_mp(own):
    have = {0: own}
    for bit in reversed(bits_of(lax.axis_size("mp"))):
        offsets = sorted(have)
        if len(offsets) == 1:
            got = [swap(have[0], "mp", bit)]
        else:
            sent = swap(jnp.stack([have[o] for o in offsets]), "mp", bit)
            got = [sent[i] for i in range(len(offsets))]
        have.update({o | bit: g for o, g in zip(offsets, got)})
    return [have[o] for o in range(len(have))]


def sum_over(x, axis, send_type):
    for bit in bits_of(lax.axis_size(axis)):
        mine = x.astype(send_type)
        x = mine.astype(f32) + swap(mine, axis, bit).astype(f32)
    return x


def dot(a, b, contract=(1, 0), precision=None):
    dims = (((contract[0],), (contract[1],)), ((), ()))
    return lax.dot_general(a, b, dims, preferred_element_type=f32, precision=precision)


def head_tail(x):
    head = x.astype(bf16)
    return head, (x - head.astype(f32)).astype(bf16)


def stacked(x):
    return jnp.concatenate(head_tail(x), axis=0)


def fold(x):
    rows = x.shape[0] // 2
    return x[:rows] + x[rows:]


def call(body, out_shape, args, scalars=(), grid=(1,), in_specs=None, out_specs=None, scratch=(), flops=0):
    moved = sum(a.size * a.dtype.itemsize for a in args)
    moved += sum(o.size * o.dtype.itemsize for o in jax.tree.leaves(out_shape))
    return kernel_call(body, out_shape, args, scalars, grid, in_specs, out_specs, scratch, flops, moved)


def kernel_call(body, out_shape, args, scalars, grid, in_specs, out_specs, scratch, flops, moved):
    return pl.pallas_call(
        body,
        out_shape=out_shape,
        grid_spec=pltpu.PrefetchScalarGridSpec(
            num_scalar_prefetch=len(scalars),
            grid=grid,
            in_specs=in_specs,
            out_specs=out_specs,
            scratch_shapes=list(scratch),
        ),
        cost_estimate=pl.CostEstimate(flops=flops, transcendentals=0, bytes_accessed=moved),
        compiler_params=pltpu.CompilerParams(vmem_limit_bytes=48 << 20),
    )(*scalars, *args)


def whole(x):
    return pl.BlockSpec(x.shape, lambda *_: (0,) * len(x.shape), pipeline_mode=pl.Buffered(1))


def tokens_of(x):
    return pl.BlockSpec((x.shape[0], TILE), lambda i, *_: (0, i))


def struct(shape, dtype):
    return jax.ShapeDtypeStruct(shape, dtype)


def prepare_kernel(count, me_ref, up_ref, down_ref, up_t_ref, down_t_ref, down_x_ref, held):
    me = me_ref[0]
    features, hidden = up_ref.shape
    piece = features // count
    strip = TILE
    for o in range(count):
        rows = pl.ds(pl.multiple_of((me ^ o) * piece, piece), piece)
        held[o * piece : (o + 1) * piece, :] = up_ref[rows, :]

    for k in range(0, hidden, strip):
        up_t_ref[k : k + strip, :] = held[:, k : k + strip].T
    for k in range(0, down_ref.shape[0], strip):
        held[:, k : k + strip] = down_ref[k : k + strip, :].T
    for o in range(count):
        rows = pl.ds(pl.multiple_of((me ^ o) * piece, piece), piece)
        down_t_ref[o * piece : (o + 1) * piece, :] = held[rows, :]
    for k in range(0, down_ref.shape[0], strip):
        down_x_ref[k : k + strip, :] = down_t_ref[:, k : k + strip].T


def prepare(w_up, w_down, me, count):
    features, hidden = w_up.shape
    outs = (struct((hidden, features), bf16), struct((features, hidden), bf16), struct((hidden, features), bf16))
    return call(
        functools.partial(prepare_kernel, count),
        outs,
        (w_up, w_down),
        (me.reshape(1),),
        in_specs=[whole(w_up), whole(w_down)],
        out_specs=[whole(o) for o in outs],
        scratch=[pltpu.VMEM((features, hidden), bf16)],
    )


def assemble(refs, held):
    at = 0
    for ref in refs:
        held[at : at + ref.shape[0], :] = ref[...]
        at += ref.shape[0]


def lanes_kept(fill_ref, block):
    return lax.broadcasted_iota(jnp.int32, (1, BLOCK), 1) < fill_ref[block]


def mask_tokens(x, fill_ref):
    per = TILE // BLOCK
    parts = []
    for b in range(per):
        keep = lanes_kept(fill_ref, pl.program_id(0) * per + b)
        part = x[:, b * BLOCK : (b + 1) * BLOCK]
        parts.append(jnp.where(keep, part, jnp.zeros_like(part)))
    return jnp.concatenate(parts, axis=1)


def forward_kernel(count, fill_ref, *refs):
    x_refs, (up_t_ref, down_t_ref), refs = refs[:count], refs[count : count + 2], refs[count + 2 :]
    hidden_ref, slope_ref, out_refs, held = refs[0], refs[1], refs[2:-1], refs[-1]
    assemble(x_refs, held)
    for k in range(0, up_t_ref.shape[0], STRIP):
        preact = dot(up_t_ref[k : k + STRIP, :], held[...])
        sig = jax.nn.sigmoid(1.702 * preact)
        active = preact * sig
        hidden_ref[k : k + STRIP, :] = active.astype(bf16)
        slope_ref[k : k + STRIP, :] = (sig + 1.702 * active * (1.0 - sig)).astype(bf16)
    piece = down_t_ref.shape[0] // count
    for o, ref in enumerate(out_refs):
        out = dot(down_t_ref[o * piece : (o + 1) * piece, :], hidden_ref[...])
        ref[...] = mask_tokens(out.astype(bf16), fill_ref)


def forward(xs, up_t, down_t, fill):
    count = len(xs)
    piece, total = xs[0].shape
    hidden, features = up_t.shape
    outs = [struct((hidden, total), bf16)] * 2 + [struct((piece, total), bf16)] * count
    got = call(
        functools.partial(forward_kernel, count),
        outs,
        (*xs, up_t, down_t),
        (fill,),
        grid=(total // TILE,),
        in_specs=[tokens_of(x) for x in xs] + [whole(up_t), whole(down_t)],
        out_specs=[tokens_of(o) for o in outs],
        scratch=[pltpu.VMEM((features, TILE), bf16)],
        flops=4 * features * hidden * total,
    )
    return got[0], got[1], got[2:]


def write_pieces(value, even_ref, odd_ref):
    half, _, piece = even_ref.shape
    for o in range(2 * half):
        part = value[:, o * piece : (o + 1) * piece]
        (odd_ref if o & 1 else even_ref)[o // 2] = part


def backward_kernel(count, fill_ref, *refs):
    c_refs, x_refs, refs = refs[:count], refs[count : 2 * count], refs[2 * count :]
    slope_ref, hidden_ref, down_x_ref, qu_ref, qd_ref = refs[:5]
    grad_ref, even_ref, odd_ref, down_ref, held_c, held_x, acc_up, acc_down = refs[5:]
    step = pl.program_id(0)

    @pl.when(step == 0)
    def _():
        acc_up[...] = jnp.zeros_like(acc_up)
        acc_down[...] = jnp.zeros_like(acc_down)

    assemble(c_refs, held_c)
    assemble(x_refs, held_x)
    held_c[...] = mask_tokens(held_c[...], fill_ref)
    for k in range(0, down_x_ref.shape[0], STRIP):
        grad = dot(down_x_ref[k : k + STRIP, :], held_c[...])
        grad_ref[k : k + STRIP, :] = (grad * slope_ref[k : k + STRIP, :].astype(f32)).astype(bf16)
    t = fold(dot(qd_ref[...], held_c[...]))
    acc_down[...] += fold(dot(stacked(t), hidden_ref[...], (1, 1)))
    u = fold(dot(qu_ref[...], grad_ref[...]))
    acc_up[...] += fold(dot(stacked(u), held_x[...], (1, 1)))

    @pl.when(step == pl.num_programs(0) - 1)
    def _():
        down_ref[...] = acc_down[...]
        write_pieces(acc_up[...], even_ref, odd_ref)


def backward(cs, xs, slope, hidden, down_x, qu, qd, fill):
    count = len(xs)
    piece, total = xs[0].shape
    units, features = down_x.shape
    rank = qu.shape[0] // 2
    pieces = struct((count // 2, rank, piece), f32)
    outs = [struct((units, total), bf16), pieces, pieces, struct((rank, units), f32)]
    return call(
        functools.partial(backward_kernel, count),
        outs,
        (*cs, *xs, slope, hidden, down_x, qu, qd),
        (fill,),
        grid=(total // TILE,),
        in_specs=[tokens_of(x) for x in (*cs, *xs, slope, hidden)] + [whole(x) for x in (down_x, qu, qd)],
        out_specs=[tokens_of(outs[0])] + [whole(o) for o in outs[1:]],
        scratch=[
            pltpu.VMEM((features, TILE), bf16),
            pltpu.VMEM((features, TILE), bf16),
            pltpu.VMEM((rank, features), f32),
            pltpu.VMEM((rank, units), f32),
        ],
        flops=2 * features * units * total,
    )


def two_sided_kernel(n_left, n_first, n_second, masked, fill_ref, *refs):
    left_refs, refs = refs[:n_left], refs[n_left:]
    first_refs, refs = refs[:n_first], refs[n_first:]
    second_refs, refs = refs[:n_second], refs[n_second:]
    out_refs, (left, first, second, acc) = refs[:-4], refs[-4:]

    @pl.when(pl.program_id(0) == 0)
    def _():
        acc[...] = jnp.zeros_like(acc)
        joined = jnp.concatenate([r[...] for r in left_refs], axis=1)
        left[...] = stacked(joined)

    assemble(first_refs, first)
    assemble(second_refs, second)
    v = fold(dot(left[...], first[...]))
    if masked:
        v = mask_tokens(v, fill_ref)
    acc[...] += fold(dot(stacked(v), second[...], (1, 1)))

    @pl.when(pl.program_id(0) == pl.num_programs(0) - 1)
    def _():
        if masked:
            write_pieces(acc[...], *out_refs)
        else:
            out_refs[0][...] = acc[...]


def two_sided(lefts, firsts, seconds, fill, masked):
    rank = lefts[0].shape[0]
    total = firsts[0].shape[1]
    inner = sum(x.shape[0] for x in firsts)
    outer = sum(x.shape[0] for x in seconds)
    if masked:
        pieces = struct((len(seconds) // 2, rank, seconds[0].shape[0]), f32)
        outs = [pieces, pieces]
    else:
        outs = [struct((rank, outer), f32)]
    return call(
        functools.partial(two_sided_kernel, len(lefts), len(firsts), len(seconds), masked),
        outs,
        (*lefts, *firsts, *seconds),
        (fill,),
        grid=(total // TILE,),
        in_specs=[whole(x) for x in lefts] + [tokens_of(x) for x in (*firsts, *seconds)],
        out_specs=[whole(o) for o in outs],
        scratch=[
            pltpu.VMEM((2 * rank, inner), bf16),
            pltpu.VMEM((inner, TILE), bf16),
            pltpu.VMEM((outer, TILE), bf16),
            pltpu.VMEM((rank, outer), f32),
        ],
        flops=4 * rank * (inner + outer) * total,
    )


def eliminate(grams):
    rank = grams[0].shape[0]
    group = 4
    wide = 2 * rank
    row = lax.broadcasted_iota(jnp.int32, (rank, wide), 0)
    column = lax.broadcasted_iota(jnp.int32, (rank, rank), 1)
    one = (lax.broadcasted_iota(jnp.int32, (rank, rank), 0) == column).astype(f32)
    state = [jnp.concatenate([g, one], axis=1) for g in grams]
    scale = [jnp.ones((rank, wide), f32) for _ in grams]
    for first in range(0, rank, group):
        columns = [
            [jnp.broadcast_to(m[:, first + k : first + k + 1], (rank, wide)) for k in range(group)]
            for m in state
        ]
        for k in range(group):
            j = first + k
            for t in range(len(grams)):
                pivot = columns[t][k][j : j + 1, :]
                factor = jnp.where(row > j, columns[t][k] * (1.0 / pivot), 0.0)
                state[t] = state[t] - factor * state[t][j : j + 1, :]
                for q in range(k + 1, group):
                    columns[t][q] = columns[t][q] - factor * columns[t][q][j : j + 1, :]
                scale[t] = jnp.where(row == j, lax.rsqrt(pivot), scale[t])
    return [(m * c)[:, rank:] for m, c in zip(state, scale)]


def factor_kernel(count, me_ref, gram_ref, down_ref, *refs):
    up_refs, outs = refs[:count], refs[count:]
    up = jnp.concatenate([r[...] for r in up_refs], axis=1)
    gram_up = dot(up, up, (1, 1), HIGHEST)
    inverses = eliminate([gram_up, gram_ref[...]])
    natural = jnp.concatenate(reorder([r[...] for r in up_refs], me_ref[0]), axis=1)
    for t, proj in enumerate((natural, down_ref[...])):
        outs[t][...] = inverses[t]
        head, tail = head_tail(dot(inverses[t], proj, precision=HIGHEST))
        outs[2 + t][...] = jnp.concatenate([head, head, tail], axis=0).T


def factor(proj_up, proj_down, gram_down, me):
    rank, units = proj_down.shape
    features = sum(p.shape[1] for p in proj_up)
    outs = [struct((rank, rank), f32)] * 2 + [struct((features, 3 * rank), bf16), struct((units, 3 * rank), bf16)]
    args = (gram_down, proj_down, *proj_up)
    return call(
        functools.partial(factor_kernel, len(proj_up)),
        outs,
        args,
        (me.reshape(1),),
        in_specs=[whole(a) for a in args],
        out_specs=[whole(o) for o in outs],
        flops=1 << 28,
    )


def outer_kernel(n_raw, me_ref, inv_ref, left_ref, *refs):
    raw_refs, (fresh_ref, approx_ref, right) = refs[:n_raw], refs[n_raw:]

    @pl.when(pl.program_id(0) == 0)
    def _():
        raw = jnp.concatenate(reorder([r[...] for r in raw_refs], me_ref[0]), axis=1)
        fresh = dot(inv_ref[...], raw, precision=HIGHEST)
        fresh_ref[...] = fresh
        head, tail = head_tail(fresh)
        right[...] = jnp.concatenate([head, tail, head], axis=0)

    approx_ref[...] = dot(left_ref[...], right[...])


def outer(inv, left, raws, me):
    rows, triple = left.shape
    columns = sum(r.shape[1] for r in raws)
    strip = 2 * BLOCK if rows % (2 * BLOCK) == 0 else BLOCK
    outs = [struct((triple // 3, columns), f32), struct((rows, columns), f32)]
    return call(
        functools.partial(outer_kernel, len(raws)),
        outs,
        (inv, left, *raws),
        (me.reshape(1),),
        grid=(rows // strip,),
        in_specs=[whole(inv), pl.BlockSpec((strip, triple), lambda i, *_: (i, 0))] + [whole(r) for r in raws],
        out_specs=[whole(outs[0]), pl.BlockSpec((strip, columns), lambda i, *_: (i, 0))],
        scratch=[pltpu.VMEM((triple, columns), bf16)],
        flops=2 * triple * rows * columns,
    )


def pack_kernel(index_ref, a_ref, b_ref, out_ref):
    for s in range(out_ref.shape[0]):
        lanes = pl.ds(pl.multiple_of(index_ref[s] * BLOCK, BLOCK), BLOCK)
        total = a_ref[:, lanes].astype(f32) + b_ref[:, lanes].astype(f32)
        out_ref[s] = total.astype(bf16)


def pack(a, b, index):
    out = struct((index.shape[0], a.shape[0], BLOCK), bf16)
    return call(pack_kernel, out, (a, b), (index,), in_specs=[whole(a), whole(b)], out_specs=whole(out))


def unpack_kernel(index_ref, ok_ref, in_ref, out_ref):
    for k in range(out_ref.shape[1] // BLOCK):
        part = in_ref[index_ref[k]]
        out_ref[:, k * BLOCK : (k + 1) * BLOCK] = jnp.where(ok_ref[k] > 0, part, jnp.zeros_like(part))


def unpack(got, index, ok):
    out = struct((got.shape[1], index.shape[0] * BLOCK), bf16)
    return call(unpack_kernel, out, (got,), (index, ok), in_specs=[whole(got)], out_specs=whole(out))


def earlier(labels):
    ids = jnp.arange(labels.shape[0], dtype=jnp.int32)
    same = (labels[:, None] == labels[None, :]) & (ids[None, :] < ids[:, None])
    return jnp.sum(same.astype(jnp.int32), axis=1)


def send_plan(ranks, ranks_dp):
    place = ranks * CAP + earlier(ranks)
    chosen = jnp.arange(ranks_dp * CAP, dtype=jnp.int32)[:, None] == place[None, :]
    ids = jnp.arange(ranks.shape[0], dtype=jnp.int32)
    return jnp.sum(jnp.where(chosen, ids[None, :], 0), axis=1).astype(jnp.int32)


def recv_plan(all_ranks, per_rank, me, most):
    total = all_ranks.shape[0]
    ids = jnp.arange(total, dtype=jnp.int32)
    source = ids // per_rank
    order = earlier(all_ranks)
    within = earlier(all_ranks + source * total)
    place = source * CAP + within
    mine = all_ranks == me
    chosen = mine[None, :] & (order[None, :] == jnp.arange(most, dtype=jnp.int32)[:, None])
    index = jnp.sum(jnp.where(chosen, place[None, :], 0), axis=1)
    return index.astype(jnp.int32), jnp.any(chosen, axis=1).astype(jnp.int32)


def all_ranks_of(ranks, me):
    count = lax.axis_size("dp")
    table = jnp.where(jnp.arange(count, dtype=jnp.int32)[:, None] == me, ranks[None, :], 0)
    for bit in bits_of(count):
        table = table + swap(table, "dp", bit)
    return table.reshape(-1)


def split_rows(x):
    head = lax.reduce_precision(x, 8, 7)
    return jnp.concatenate([head.astype(bf16), (x - head).astype(bf16)], axis=0)


def local(patches, cotangent, encoder_rank, block_fill, w_up, w_down, q_up, q_down):
    ranks_dp = lax.axis_size("dp")
    count = lax.axis_size("mp")
    me, me_dp = lax.axis_index("mp"), lax.axis_index("dp")
    blocks = encoder_rank.shape[0]

    xs = gather_xor(patches.T)
    cs = gather_xor(cotangent.T)
    every = all_ranks_of(encoder_rank, me_dp)
    up_t, down_t, down_x = prepare(w_up, w_down, me, count)
    qd = split_rows(jnp.concatenate(reorder(slices(q_down.T, count, 1), me), axis=1))
    qu = split_rows(q_up.T)

    hidden, slope, outs = forward(xs, up_t, down_t, block_fill)
    grad_pre, even, odd, proj_down = backward(cs, xs, slope, hidden, down_x, qu, qd, block_fill)

    have = {o: outs[o].astype(f32) for o in range(0, count, 2)}
    have = {o: (h + swap(outs[o | 1], "mp", 1).astype(f32)).astype(bf16) for o, h in have.items()}
    for bit in bits_of(count)[1:]:
        got = {o ^ bit: swap(have[o], "mp", bit) for o in have if o & bit}
        if len(got) == 1:
            break
        have = {o: (have[o].astype(f32) + got[o].astype(f32)).astype(bf16) for o in got}
    sent = pack(have[0], got[0], send_plan(encoder_rank, ranks_dp))
    received = lax.all_to_all(sent, "dp", split_axis=0, concat_axis=0, tiled=True)
    encoded = unpack(received, *recv_plan(every, blocks, me_dp, blocks + EXTRA))

    proj_down = sum_over(proj_down, "dp", bf16)
    proj_up = sum_over(reduce_mp(even, odd), "dp", f32)
    proj_up = spread_mp(proj_up)

    even, odd = two_sided([proj_down], [hidden], cs, block_fill, True)
    (raw_up,) = two_sided(proj_up, xs, [grad_pre], block_fill, False)

    gram_down = sum_over(dot(proj_down, proj_down, (1, 1), HIGHEST), "mp", f32)
    inv_up, inv_down, left_up, left_down = factor(proj_up, proj_down, gram_down, me)

    raw_down = sum_over(reduce_mp(even, odd), "dp", f32)
    raw_up = sum_over(raw_up, "dp", bf16)
    raw_down = spread_mp(raw_down)
    fresh_up, approx_up = outer(inv_up, left_up, [raw_up], me)
    fresh_down, approx_down = outer(inv_down, left_down, raw_down, me)
    return (encoded.T, approx_up, approx_down, fresh_up.T, fresh_down.T)


def solution(mesh):
    placed = (
        P("dp", "mp"),
        P("dp", "mp"),
        P("dp"),
        P("dp"),
        P(None, "mp"),
        P("mp", None),
        P("mp", None),
        P(),
    )
    return jax.shard_map(
        local,
        mesh=mesh,
        in_specs=placed,
        out_specs=(P("dp", "mp"), P(None, "mp"), P("mp", None), P("mp", None), P()),
        check_vma=False,
    )
```

```python
import functools

import jax
import jax.numpy as jnp
from jax import lax
from jax.experimental import pallas as pl
from jax.experimental.pallas import tpu as pltpu
from jax.sharding import PartitionSpec as P


BLOCK = 128
TILE = 512
STRIP = 128
CAP = 2
EXTRA = 6
FLAG = 16
bf16 = jnp.bfloat16
f32 = jnp.float32
HIGHEST = lax.Precision.HIGHEST


def bits_of(count):
    return [1 << b for b in range(count.bit_length() - 1)]


def swap(x, axis, bit):
    count = lax.axis_size(axis)
    return lax.ppermute(x, axis, [(i, i ^ bit) for i in range(count)])


def gather_xor(own):
    count = lax.axis_size("mp")
    pieces = {0: own}
    for bit in bits_of(count)[1:]:
        pieces.update({o | bit: swap(p, "mp", bit) for o, p in list(pieces.items())})
    near = {o | 1: swap(p, "mp", 1) for o, p in pieces.items()}
    pieces.update(near)
    return [pieces[o] for o in range(count)]


def reorder(pieces, me):
    for bit in bits_of(len(pieces)):
        flip = (me & bit) != 0
        pieces = [jnp.where(flip, pieces[i ^ bit], pieces[i]) for i in range(len(pieces))]
    return pieces


def slices(x, count, axis):
    size = x.shape[axis] // count
    return [lax.slice_in_dim(x, i * size, (i + 1) * size, axis=axis) for i in range(count)]


def reduce_mp(even, odd):
    have = even + swap(odd, "mp", 1)
    for bit in bits_of(lax.axis_size("mp"))[1:]:
        have = have.reshape(have.shape[0] // 2, 2, *have.shape[1:])
        have = have[:, 0] + swap(have[:, 1], "mp", bit)
    return have[0]


def spread_mp(own):
    have = {0: own}
    for bit in reversed(bits_of(lax.axis_size("mp"))):
        offsets = sorted(have)
        if len(offsets) == 1:
            got = [swap(have[0], "mp", bit)]
        else:
            sent = swap(jnp.stack([have[o] for o in offsets]), "mp", bit)
            got = [sent[i] for i in range(len(offsets))]
        have.update({o | bit: g for o, g in zip(offsets, got)})
    return [have[o] for o in range(len(have))]


def sum_over(x, axis, send_type):
    for bit in bits_of(lax.axis_size(axis)):
        mine = x.astype(send_type)
        x = mine.astype(f32) + swap(mine, axis, bit).astype(f32)
    return x


def dot(a, b, contract=(1, 0), precision=None):
    dims = (((contract[0],), (contract[1],)), ((), ()))
    return lax.dot_general(a, b, dims, preferred_element_type=f32, precision=precision)


def head_tail(x):
    head = x.astype(bf16)
    return head, (x - head.astype(f32)).astype(bf16)


def stacked(x):
    return jnp.concatenate(head_tail(x), axis=0)


def fold(x):
    rows = x.shape[0] // 2
    return x[:rows] + x[rows:]


def call(body, out_shape, args, scalars=(), grid=(1,), in_specs=None, out_specs=None, scratch=(), flops=0):
    moved = sum(a.size * a.dtype.itemsize for a in args)
    moved += sum(o.size * o.dtype.itemsize for o in jax.tree.leaves(out_shape))
    return kernel_call(body, out_shape, args, scalars, grid, in_specs, out_specs, scratch, flops, moved)


def kernel_call(body, out_shape, args, scalars, grid, in_specs, out_specs, scratch, flops, moved):
    return pl.pallas_call(
        body,
        out_shape=out_shape,
        grid_spec=pltpu.PrefetchScalarGridSpec(
            num_scalar_prefetch=len(scalars),
            grid=grid,
            in_specs=in_specs,
            out_specs=out_specs,
            scratch_shapes=list(scratch),
        ),
        cost_estimate=pl.CostEstimate(flops=flops, transcendentals=0, bytes_accessed=moved),
        compiler_params=pltpu.CompilerParams(vmem_limit_bytes=48 << 20),
    )(*scalars, *args)


def whole(x):
    return pl.BlockSpec(x.shape, lambda *_: (0,) * len(x.shape), pipeline_mode=pl.Buffered(1))


def tokens_of(x):
    return pl.BlockSpec((x.shape[0], TILE), lambda i, *_: (0, i))


def struct(shape, dtype):
    return jax.ShapeDtypeStruct(shape, dtype)


def prepare_kernel(count, me_ref, up_ref, down_ref, up_t_ref, down_t_ref, down_x_ref, held):
    me = me_ref[0]
    features, hidden = up_ref.shape
    piece = features // count
    strip = TILE
    for o in range(count):
        rows = pl.ds(pl.multiple_of((me ^ o) * piece, piece), piece)
        held[o * piece : (o + 1) * piece, :] = up_ref[rows, :]

    for k in range(0, hidden, strip):
        up_t_ref[k : k + strip, :] = held[:, k : k + strip].T
    for k in range(0, down_ref.shape[0], strip):
        held[:, k : k + strip] = down_ref[k : k + strip, :].T
    for o in range(count):
        rows = pl.ds(pl.multiple_of((me ^ o) * piece, piece), piece)
        down_t_ref[o * piece : (o + 1) * piece, :] = held[rows, :]
    for k in range(0, down_ref.shape[0], strip):
        down_x_ref[k : k + strip, :] = down_t_ref[:, k : k + strip].T


def prepare(w_up, w_down, me, count):
    features, hidden = w_up.shape
    outs = (struct((hidden, features), bf16), struct((features, hidden), bf16), struct((hidden, features), bf16))
    return call(
        functools.partial(prepare_kernel, count),
        outs,
        (w_up, w_down),
        (me.reshape(1),),
        in_specs=[whole(w_up), whole(w_down)],
        out_specs=[whole(o) for o in outs],
        scratch=[pltpu.VMEM((features, hidden), bf16)],
    )


def assemble(refs, held):
    at = 0
    for ref in refs:
        held[at : at + ref.shape[0], :] = ref[...]
        at += ref.shape[0]


def lanes_kept(fill_ref, block):
    return lax.broadcasted_iota(jnp.int32, (1, BLOCK), 1) < fill_ref[block]


def mask_tokens(x, fill_ref):
    per = TILE // BLOCK
    parts = []
    for b in range(per):
        keep = lanes_kept(fill_ref, pl.program_id(0) * per + b)
        part = x[:, b * BLOCK : (b + 1) * BLOCK]
        parts.append(jnp.where(keep, part, jnp.zeros_like(part)))
    return jnp.concatenate(parts, axis=1)


def forward_kernel(count, fill_ref, *refs):
    x_refs, (up_t_ref, down_t_ref), refs = refs[:count], refs[count : count + 2], refs[count + 2 :]
    hidden_ref, slope_ref, out_refs, held = refs[0], refs[1], refs[2:-1], refs[-1]
    assemble(x_refs, held)
    for k in range(0, up_t_ref.shape[0], STRIP):
        preact = dot(up_t_ref[k : k + STRIP, :], held[...])
        sig = jax.nn.sigmoid(1.702 * preact)
        active = preact * sig
        hidden_ref[k : k + STRIP, :] = active.astype(bf16)
        slope_ref[k : k + STRIP, :] = (sig + 1.702 * active * (1.0 - sig)).astype(bf16)
    piece = down_t_ref.shape[0] // count
    for o, ref in enumerate(out_refs):
        out = dot(down_t_ref[o * piece : (o + 1) * piece, :], hidden_ref[...])
        ref[...] = mask_tokens(out.astype(bf16), fill_ref)


def forward(xs, up_t, down_t, fill):
    count = len(xs)
    piece, total = xs[0].shape
    hidden, features = up_t.shape
    outs = [struct((hidden, total), bf16)] * 2 + [struct((piece, total), bf16)] * count
    got = call(
        functools.partial(forward_kernel, count),
        outs,
        (*xs, up_t, down_t),
        (fill,),
        grid=(total // TILE,),
        in_specs=[tokens_of(x) for x in xs] + [whole(up_t), whole(down_t)],
        out_specs=[tokens_of(o) for o in outs],
        scratch=[pltpu.VMEM((features, TILE), bf16)],
        flops=4 * features * hidden * total,
    )
    return got[0], got[1], got[2:]


def write_pieces(value, even_ref, odd_ref):
    half, _, piece = even_ref.shape
    for o in range(2 * half):
        part = value[:, o * piece : (o + 1) * piece]
        (odd_ref if o & 1 else even_ref)[o // 2] = part


def backward_kernel(count, fill_ref, *refs):
    c_refs, x_refs, refs = refs[:count], refs[count : 2 * count], refs[2 * count :]
    slope_ref, hidden_ref, down_x_ref, qu_ref, qd_ref = refs[:5]
    grad_ref, even_ref, odd_ref, down_ref, held_c, held_x, acc_up, acc_down = refs[5:]
    step = pl.program_id(0)

    @pl.when(step == 0)
    def _():
        acc_up[...] = jnp.zeros_like(acc_up)
        acc_down[...] = jnp.zeros_like(acc_down)

    assemble(c_refs, held_c)
    assemble(x_refs, held_x)
    held_c[...] = mask_tokens(held_c[...], fill_ref)
    for k in range(0, down_x_ref.shape[0], STRIP):
        grad = dot(down_x_ref[k : k + STRIP, :], held_c[...])
        grad_ref[k : k + STRIP, :] = (grad * slope_ref[k : k + STRIP, :].astype(f32)).astype(bf16)
    t = fold(dot(qd_ref[...], held_c[...]))
    acc_down[...] += fold(dot(stacked(t), hidden_ref[...], (1, 1)))
    u = fold(dot(qu_ref[...], grad_ref[...]))
    acc_up[...] += fold(dot(stacked(u), held_x[...], (1, 1)))

    @pl.when(step == pl.num_programs(0) - 1)
    def _():
        down_ref[...] = acc_down[...]
        write_pieces(acc_up[...], even_ref, odd_ref)


def backward(cs, xs, slope, hidden, down_x, qu, qd, fill):
    count = len(xs)
    piece, total = xs[0].shape
    units, features = down_x.shape
    rank = qu.shape[0] // 2
    pieces = struct((count // 2, rank, piece), f32)
    outs = [struct((units, total), bf16), pieces, pieces, struct((rank, units), f32)]
    return call(
        functools.partial(backward_kernel, count),
        outs,
        (*cs, *xs, slope, hidden, down_x, qu, qd),
        (fill,),
        grid=(total // TILE,),
        in_specs=[tokens_of(x) for x in (*cs, *xs, slope, hidden)] + [whole(x) for x in (down_x, qu, qd)],
        out_specs=[tokens_of(outs[0])] + [whole(o) for o in outs[1:]],
        scratch=[
            pltpu.VMEM((features, TILE), bf16),
            pltpu.VMEM((features, TILE), bf16),
            pltpu.VMEM((rank, features), f32),
            pltpu.VMEM((rank, units), f32),
        ],
        flops=2 * features * units * total,
    )


def two_sided_kernel(n_left, n_first, n_second, masked, fill_ref, *refs):
    left_refs, refs = refs[:n_left], refs[n_left:]
    first_refs, refs = refs[:n_first], refs[n_first:]
    second_refs, refs = refs[:n_second], refs[n_second:]
    out_refs, (left, first, second, acc) = refs[:-4], refs[-4:]

    @pl.when(pl.program_id(0) == 0)
    def _():
        acc[...] = jnp.zeros_like(acc)
        joined = jnp.concatenate([r[...] for r in left_refs], axis=1)
        left[...] = stacked(joined)

    assemble(first_refs, first)
    assemble(second_refs, second)
    v = fold(dot(left[...], first[...]))
    if masked:
        v = mask_tokens(v, fill_ref)
    acc[...] += fold(dot(stacked(v), second[...], (1, 1)))

    @pl.when(pl.program_id(0) == pl.num_programs(0) - 1)
    def _():
        if masked:
            write_pieces(acc[...], *out_refs)
        else:
            out_refs[0][...] = acc[...]


def two_sided(lefts, firsts, seconds, fill, masked):
    rank = lefts[0].shape[0]
    total = firsts[0].shape[1]
    inner = sum(x.shape[0] for x in firsts)
    outer = sum(x.shape[0] for x in seconds)
    if masked:
        pieces = struct((len(seconds) // 2, rank, seconds[0].shape[0]), f32)
        outs = [pieces, pieces]
    else:
        outs = [struct((rank, outer), f32)]
    return call(
        functools.partial(two_sided_kernel, len(lefts), len(firsts), len(seconds), masked),
        outs,
        (*lefts, *firsts, *seconds),
        (fill,),
        grid=(total // TILE,),
        in_specs=[whole(x) for x in lefts] + [tokens_of(x) for x in (*firsts, *seconds)],
        out_specs=[whole(o) for o in outs],
        scratch=[
            pltpu.VMEM((2 * rank, inner), bf16),
            pltpu.VMEM((inner, TILE), bf16),
            pltpu.VMEM((outer, TILE), bf16),
            pltpu.VMEM((rank, outer), f32),
        ],
        flops=4 * rank * (inner + outer) * total,
    )


def eliminate(grams):
    rank = grams[0].shape[0]
    group = 4
    wide = 2 * rank
    row = lax.broadcasted_iota(jnp.int32, (rank, wide), 0)
    column = lax.broadcasted_iota(jnp.int32, (rank, rank), 1)
    one = (lax.broadcasted_iota(jnp.int32, (rank, rank), 0) == column).astype(f32)
    state = [jnp.concatenate([g, one], axis=1) for g in grams]
    scale = [jnp.ones((rank, wide), f32) for _ in grams]
    for first in range(0, rank, group):
        columns = [
            [jnp.broadcast_to(m[:, first + k : first + k + 1], (rank, wide)) for k in range(group)]
            for m in state
        ]
        for k in range(group):
            j = first + k
            for t in range(len(grams)):
                pivot = columns[t][k][j : j + 1, :]
                factor = jnp.where(row > j, columns[t][k] * (1.0 / pivot), 0.0)
                state[t] = state[t] - factor * state[t][j : j + 1, :]
                for q in range(k + 1, group):
                    columns[t][q] = columns[t][q] - factor * columns[t][q][j : j + 1, :]
                scale[t] = jnp.where(row == j, lax.rsqrt(pivot), scale[t])
    return [(m * c)[:, rank:] for m, c in zip(state, scale)]


def factor_kernel(count, me_ref, gram_ref, down_ref, *refs):
    up_refs, outs = refs[:count], refs[count:]
    up = jnp.concatenate([r[...] for r in up_refs], axis=1)
    gram_up = dot(up, up, (1, 1), HIGHEST)
    inverses = eliminate([gram_up, gram_ref[...]])
    natural = jnp.concatenate(reorder([r[...] for r in up_refs], me_ref[0]), axis=1)
    for t, proj in enumerate((natural, down_ref[...])):
        outs[t][...] = inverses[t]
        head, tail = head_tail(dot(inverses[t], proj, precision=HIGHEST))
        outs[2 + t][...] = jnp.concatenate([head, head, tail], axis=0).T


def factor(proj_up, proj_down, gram_down, me):
    rank, units = proj_down.shape
    features = sum(p.shape[1] for p in proj_up)
    outs = [struct((rank, rank), f32)] * 2 + [struct((features, 3 * rank), bf16), struct((units, 3 * rank), bf16)]
    args = (gram_down, proj_down, *proj_up)
    return call(
        functools.partial(factor_kernel, len(proj_up)),
        outs,
        args,
        (me.reshape(1),),
        in_specs=[whole(a) for a in args],
        out_specs=[whole(o) for o in outs],
        flops=1 << 28,
    )


def outer_kernel(n_raw, me_ref, inv_ref, left_ref, *refs):
    raw_refs, (fresh_ref, approx_ref, right) = refs[:n_raw], refs[n_raw:]

    @pl.when(pl.program_id(0) == 0)
    def _():
        raw = jnp.concatenate(reorder([r[...] for r in raw_refs], me_ref[0]), axis=1)
        fresh = dot(inv_ref[...], raw, precision=HIGHEST)
        fresh_ref[...] = fresh
        head, tail = head_tail(fresh)
        right[...] = jnp.concatenate([head, tail, head], axis=0)

    approx_ref[...] = dot(left_ref[...], right[...])


def outer(inv, left, raws, me):
    rows, triple = left.shape
    columns = sum(r.shape[1] for r in raws)
    strip = 2 * BLOCK if rows % (2 * BLOCK) == 0 else BLOCK
    outs = [struct((triple // 3, columns), f32), struct((rows, columns), f32)]
    return call(
        functools.partial(outer_kernel, len(raws)),
        outs,
        (inv, left, *raws),
        (me.reshape(1),),
        grid=(rows // strip,),
        in_specs=[whole(inv), pl.BlockSpec((strip, triple), lambda i, *_: (i, 0))] + [whole(r) for r in raws],
        out_specs=[whole(outs[0]), pl.BlockSpec((strip, columns), lambda i, *_: (i, 0))],
        scratch=[pltpu.VMEM((triple, columns), bf16)],
        flops=2 * triple * rows * columns,
    )


def pack_kernel(index_ref, ok_ref, a_ref, b_ref, out_ref):
    piece = a_ref.shape[0]
    for s in range(out_ref.shape[0]):
        lanes = pl.ds(pl.multiple_of(index_ref[s] * BLOCK, BLOCK), BLOCK)
        total = a_ref[:, lanes].astype(f32) + b_ref[:, lanes].astype(f32)
        out_ref[s, :piece, :] = total.astype(bf16)
        out_ref[s, piece:, :] = jnp.full((FLAG, BLOCK), ok_ref[s].astype(f32)).astype(bf16)


def pack(a, b, index, ok):
    out = struct((index.shape[0], a.shape[0] + FLAG, BLOCK), bf16)
    return call(pack_kernel, out, (a, b), (index, ok), in_specs=[whole(a), whole(b)], out_specs=whole(out))


def unpack_kernel(in_ref, out_ref):
    piece = out_ref.shape[0]
    out_ref[...] = jnp.zeros_like(out_ref)
    used = [jnp.max(in_ref[s, piece:, :].astype(f32)).astype(jnp.int32) for s in range(in_ref.shape[0])]
    at = jnp.int32(0)
    for s, one in enumerate(used):

        @pl.when(one > 0)
        def _(s=s, at=at):
            lanes = pl.ds(pl.multiple_of(at * BLOCK, BLOCK), BLOCK)
            out_ref[:, lanes] = in_ref[s, :piece, :]

        at = at + one


def unpack(got, most):
    out = struct((got.shape[1] - FLAG, most * BLOCK), bf16)
    return call(unpack_kernel, out, (got,), in_specs=[whole(got)], out_specs=whole(out))


def earlier(labels):
    ids = jnp.arange(labels.shape[0], dtype=jnp.int32)
    same = (labels[:, None] == labels[None, :]) & (ids[None, :] < ids[:, None])
    return jnp.sum(same.astype(jnp.int32), axis=1)


def send_plan(ranks, ranks_dp):
    place = ranks * CAP + earlier(ranks)
    chosen = jnp.arange(ranks_dp * CAP, dtype=jnp.int32)[:, None] == place[None, :]
    ids = jnp.arange(ranks.shape[0], dtype=jnp.int32)
    index = jnp.sum(jnp.where(chosen, ids[None, :], 0), axis=1)
    return index.astype(jnp.int32), jnp.any(chosen, axis=1).astype(jnp.int32)


def split_rows(x):
    head = lax.reduce_precision(x, 8, 7)
    return jnp.concatenate([head.astype(bf16), (x - head).astype(bf16)], axis=0)


def local(patches, cotangent, encoder_rank, block_fill, w_up, w_down, q_up, q_down):
    ranks_dp = lax.axis_size("dp")
    count = lax.axis_size("mp")
    me = lax.axis_index("mp")
    blocks = encoder_rank.shape[0]

    xs = gather_xor(patches.T)
    cs = gather_xor(cotangent.T)
    up_t, down_t, down_x = prepare(w_up, w_down, me, count)
    qd = split_rows(jnp.concatenate(reorder(slices(q_down.T, count, 1), me), axis=1))
    qu = split_rows(q_up.T)

    hidden, slope, outs = forward(xs, up_t, down_t, block_fill)
    grad_pre, even, odd, proj_down = backward(cs, xs, slope, hidden, down_x, qu, qd, block_fill)

    have = {o: outs[o].astype(f32) for o in range(0, count, 2)}
    have = {o: (h + swap(outs[o | 1], "mp", 1).astype(f32)).astype(bf16) for o, h in have.items()}
    for bit in bits_of(count)[1:]:
        got = {o ^ bit: swap(have[o], "mp", bit) for o in have if o & bit}
        if len(got) == 1:
            break
        have = {o: (have[o].astype(f32) + got[o].astype(f32)).astype(bf16) for o in got}
    sent = pack(have[0], got[0], *send_plan(encoder_rank, ranks_dp))
    received = lax.all_to_all(sent, "dp", split_axis=0, concat_axis=0, tiled=True)
    encoded = unpack(received, blocks + EXTRA)

    proj_down = sum_over(proj_down, "dp", bf16)
    proj_up = sum_over(reduce_mp(even, odd), "dp", f32)
    proj_up = spread_mp(proj_up)

    even, odd = two_sided([proj_down], [hidden], cs, block_fill, True)
    (raw_up,) = two_sided(proj_up, xs, [grad_pre], block_fill, False)

    gram_down = sum_over(dot(proj_down, proj_down, (1, 1), HIGHEST), "mp", f32)
    inv_up, inv_down, left_up, left_down = factor(proj_up, proj_down, gram_down, me)

    raw_down = sum_over(reduce_mp(even, odd), "dp", f32)
    raw_up = sum_over(raw_up, "dp", bf16)
    raw_down = spread_mp(raw_down)
    fresh_up, approx_up = outer(inv_up, left_up, [raw_up], me)
    fresh_down, approx_down = outer(inv_down, left_down, raw_down, me)
    return (encoded.T, approx_up, approx_down, fresh_up.T, fresh_down.T)


def solution(mesh):
    placed = (
        P("dp", "mp"),
        P("dp", "mp"),
        P("dp"),
        P("dp"),
        P(None, "mp"),
        P("mp", None),
        P("mp", None),
        P(),
    )
    return jax.shard_map(
        local,
        mesh=mesh,
        in_specs=placed,
        out_specs=(P("dp", "mp"), P(None, "mp"), P("mp", None), P("mp", None), P()),
        check_vma=False,
    )
```

```python
import functools

import jax
import jax.numpy as jnp
from jax import lax
from jax.experimental import pallas as pl
from jax.experimental.pallas import tpu as pltpu
from jax.sharding import PartitionSpec as P


BLOCK = 128
TILE = 512
STRIP = 128
CAP = 2
EXTRA = 6
FLAG = 16
bf16 = jnp.bfloat16
f32 = jnp.float32
HIGHEST = lax.Precision.HIGHEST


def bits_of(count):
    return [1 << b for b in range(count.bit_length() - 1)]


def swap(x, axis, bit):
    count = lax.axis_size(axis)
    return lax.ppermute(x, axis, [(i, i ^ bit) for i in range(count)])


def gather_xor(own):
    count = lax.axis_size("mp")
    pieces = {0: own}
    for bit in bits_of(count)[1:]:
        pieces.update({o | bit: swap(p, "mp", bit) for o, p in list(pieces.items())})
    near = {o | 1: swap(p, "mp", 1) for o, p in pieces.items()}
    pieces.update(near)
    return [pieces[o] for o in range(count)]


def reorder(pieces, me):
    for bit in bits_of(len(pieces)):
        flip = (me & bit) != 0
        pieces = [jnp.where(flip, pieces[i ^ bit], pieces[i]) for i in range(len(pieces))]
    return pieces


def slices(x, count, axis):
    size = x.shape[axis] // count
    return [lax.slice_in_dim(x, i * size, (i + 1) * size, axis=axis) for i in range(count)]


def reduce_mp(even, odd):
    have = even + swap(odd, "mp", 1)
    for bit in bits_of(lax.axis_size("mp"))[1:]:
        have = have.reshape(have.shape[0] // 2, 2, *have.shape[1:])
        have = have[:, 0] + swap(have[:, 1], "mp", bit)
    return have[0]


def spread_mp(own):
    have = {0: own}
    for bit in reversed(bits_of(lax.axis_size("mp"))):
        offsets = sorted(have)
        if len(offsets) == 1:
            got = [swap(have[0], "mp", bit)]
        else:
            sent = swap(jnp.stack([have[o] for o in offsets]), "mp", bit)
            got = [sent[i] for i in range(len(offsets))]
        have.update({o | bit: g for o, g in zip(offsets, got)})
    return [have[o] for o in range(len(have))]


def sum_over(x, axis, send_type):
    for bit in bits_of(lax.axis_size(axis)):
        mine = x.astype(send_type)
        x = mine.astype(f32) + swap(mine, axis, bit).astype(f32)
    return x


def dot(a, b, contract=(1, 0), precision=None):
    dims = (((contract[0],), (contract[1],)), ((), ()))
    return lax.dot_general(a, b, dims, preferred_element_type=f32, precision=precision)


def head_tail(x):
    head = x.astype(bf16)
    return head, (x - head.astype(f32)).astype(bf16)


def stacked(x):
    return jnp.concatenate(head_tail(x), axis=0)


def fold(x):
    rows = x.shape[0] // 2
    return x[:rows] + x[rows:]


def call(body, out_shape, args, scalars=(), grid=(1,), in_specs=None, out_specs=None, scratch=(), flops=0):
    moved = sum(a.size * a.dtype.itemsize for a in args)
    moved += sum(o.size * o.dtype.itemsize for o in jax.tree.leaves(out_shape))
    return kernel_call(body, out_shape, args, scalars, grid, in_specs, out_specs, scratch, flops, moved)


def kernel_call(body, out_shape, args, scalars, grid, in_specs, out_specs, scratch, flops, moved):
    return pl.pallas_call(
        body,
        out_shape=out_shape,
        grid_spec=pltpu.PrefetchScalarGridSpec(
            num_scalar_prefetch=len(scalars),
            grid=grid,
            in_specs=in_specs,
            out_specs=out_specs,
            scratch_shapes=list(scratch),
        ),
        cost_estimate=pl.CostEstimate(flops=flops, transcendentals=0, bytes_accessed=moved),
        compiler_params=pltpu.CompilerParams(vmem_limit_bytes=48 << 20),
    )(*scalars, *args)


def whole(x):
    return pl.BlockSpec(x.shape, lambda *_: (0,) * len(x.shape), pipeline_mode=pl.Buffered(1))


def tokens_of(x):
    return pl.BlockSpec((x.shape[0], TILE), lambda i, *_: (0, i))


def struct(shape, dtype):
    return jax.ShapeDtypeStruct(shape, dtype)


def prepare_kernel(count, me_ref, up_ref, down_ref, up_t_ref, down_t_ref, down_x_ref, held):
    me = me_ref[0]
    features, hidden = up_ref.shape
    piece = features // count
    strip = TILE
    for o in range(count):
        rows = pl.ds(pl.multiple_of((me ^ o) * piece, piece), piece)
        held[o * piece : (o + 1) * piece, :] = up_ref[rows, :]

    for k in range(0, hidden, strip):
        up_t_ref[k : k + strip, :] = held[:, k : k + strip].T
    for k in range(0, down_ref.shape[0], strip):
        held[:, k : k + strip] = down_ref[k : k + strip, :].T
    for o in range(count):
        rows = pl.ds(pl.multiple_of((me ^ o) * piece, piece), piece)
        down_t_ref[o * piece : (o + 1) * piece, :] = held[rows, :]
    for k in range(0, down_ref.shape[0], strip):
        down_x_ref[k : k + strip, :] = down_t_ref[:, k : k + strip].T


def prepare(w_up, w_down, me, count):
    features, hidden = w_up.shape
    outs = (struct((hidden, features), bf16), struct((features, hidden), bf16), struct((hidden, features), bf16))
    return call(
        functools.partial(prepare_kernel, count),
        outs,
        (w_up, w_down),
        (me.reshape(1),),
        in_specs=[whole(w_up), whole(w_down)],
        out_specs=[whole(o) for o in outs],
        scratch=[pltpu.VMEM((features, hidden), bf16)],
    )


def assemble(refs, held):
    at = 0
    for ref in refs:
        held[at : at + ref.shape[0], :] = ref[...]
        at += ref.shape[0]


def joined(refs, held):
    if len(refs) == 1:
        return refs[0]
    assemble(refs, held)
    return held


def lanes_kept(fill_ref, block):
    return lax.broadcasted_iota(jnp.int32, (1, BLOCK), 1) < fill_ref[block]


def mask_tokens(x, fill_ref):
    per = x.shape[1] // BLOCK
    parts = []
    for b in range(per):
        keep = lanes_kept(fill_ref, pl.program_id(0) * per + b)
        part = x[:, b * BLOCK : (b + 1) * BLOCK]
        parts.append(jnp.where(keep, part, jnp.zeros_like(part)))
    return jnp.concatenate(parts, axis=1)


def forward_kernel(count, fill_ref, *refs):
    x_refs, (up_t_ref, down_t_ref), refs = refs[:count], refs[count : count + 2], refs[count + 2 :]
    hidden_ref, slope_ref, out_refs, held = refs[0], refs[1], refs[2:-1], refs[-1]
    assemble(x_refs, held)
    for k in range(0, up_t_ref.shape[0], STRIP):
        preact = dot(up_t_ref[k : k + STRIP, :], held[...])
        sig = jax.nn.sigmoid(1.702 * preact)
        active = preact * sig
        hidden_ref[k : k + STRIP, :] = active.astype(bf16)
        slope_ref[k : k + STRIP, :] = (sig + 1.702 * active * (1.0 - sig)).astype(bf16)
    piece = down_t_ref.shape[0] // count
    for o, ref in enumerate(out_refs):
        out = dot(down_t_ref[o * piece : (o + 1) * piece, :], hidden_ref[...])
        ref[...] = mask_tokens(out.astype(bf16), fill_ref)


def forward(xs, up_t, down_t, fill):
    count = len(xs)
    piece, total = xs[0].shape
    hidden, features = up_t.shape
    outs = [struct((hidden, total), bf16)] * 2 + [struct((piece, total), bf16)] * count
    got = call(
        functools.partial(forward_kernel, count),
        outs,
        (*xs, up_t, down_t),
        (fill,),
        grid=(total // TILE,),
        in_specs=[tokens_of(x) for x in xs] + [whole(up_t), whole(down_t)],
        out_specs=[tokens_of(o) for o in outs],
        scratch=[pltpu.VMEM((features, TILE), bf16)],
        flops=4 * features * hidden * total,
    )
    return got[0], got[1], got[2:]


def write_pieces(value, even_ref, odd_ref):
    half, _, piece = even_ref.shape
    for o in range(2 * half):
        part = value[:, o * piece : (o + 1) * piece]
        (odd_ref if o & 1 else even_ref)[o // 2] = part


def backward_kernel(count, fill_ref, *refs):
    c_refs, x_refs, refs = refs[:count], refs[count : 2 * count], refs[2 * count :]
    slope_ref, hidden_ref, down_x_ref, qu_ref, qd_ref = refs[:5]
    grad_ref, even_ref, odd_ref, down_ref, held_c, held_x, acc_up, acc_down = refs[5:]
    step = pl.program_id(0)

    @pl.when(step == 0)
    def _():
        acc_up[...] = jnp.zeros_like(acc_up)
        acc_down[...] = jnp.zeros_like(acc_down)

    assemble(c_refs, held_c)
    assemble(x_refs, held_x)
    held_c[...] = mask_tokens(held_c[...], fill_ref)
    for k in range(0, down_x_ref.shape[0], STRIP):
        grad = dot(down_x_ref[k : k + STRIP, :], held_c[...])
        grad_ref[k : k + STRIP, :] = (grad * slope_ref[k : k + STRIP, :].astype(f32)).astype(bf16)
    t = fold(dot(qd_ref[...], held_c[...]))
    acc_down[...] += fold(dot(stacked(t), hidden_ref[...], (1, 1)))
    u = fold(dot(qu_ref[...], grad_ref[...]))
    acc_up[...] += fold(dot(stacked(u), held_x[...], (1, 1)))

    @pl.when(step == pl.num_programs(0) - 1)
    def _():
        down_ref[...] = acc_down[...]
        write_pieces(acc_up[...], even_ref, odd_ref)


def backward(cs, xs, slope, hidden, down_x, qu, qd, fill):
    count = len(xs)
    piece, total = xs[0].shape
    units, features = down_x.shape
    rank = qu.shape[0] // 2
    pieces = struct((count // 2, rank, piece), f32)
    outs = [struct((units, total), bf16), pieces, pieces, struct((rank, units), f32)]
    return call(
        functools.partial(backward_kernel, count),
        outs,
        (*cs, *xs, slope, hidden, down_x, qu, qd),
        (fill,),
        grid=(total // TILE,),
        in_specs=[tokens_of(x) for x in (*cs, *xs, slope, hidden)] + [whole(x) for x in (down_x, qu, qd)],
        out_specs=[tokens_of(outs[0])] + [whole(o) for o in outs[1:]],
        scratch=[
            pltpu.VMEM((features, TILE), bf16),
            pltpu.VMEM((features, TILE), bf16),
            pltpu.VMEM((rank, features), f32),
            pltpu.VMEM((rank, units), f32),
        ],
        flops=2 * features * units * total,
    )


def two_sided_kernel(n_left, n_first, n_second, masked, fill_ref, *refs):
    left_refs, refs = refs[:n_left], refs[n_left:]
    first_refs, refs = refs[:n_first], refs[n_first:]
    second_refs, refs = refs[:n_second], refs[n_second:]
    out_refs, (left, first, second) = refs[:-3], refs[-3:]
    left[...] = stacked(jnp.concatenate([r[...] for r in left_refs], axis=1))
    first, second = joined(first_refs, first), joined(second_refs, second)
    v = fold(dot(left[...], first[...]))
    if masked:
        v = mask_tokens(v, fill_ref)
    product = fold(dot(stacked(v), second[...], (1, 1)))
    if masked:
        write_pieces(product, *out_refs)
    else:
        out_refs[0][...] = product


def two_sided(lefts, firsts, seconds, fill, masked):
    rank = lefts[0].shape[0]
    total = firsts[0].shape[1]
    inner = sum(x.shape[0] for x in firsts)
    outer = sum(x.shape[0] for x in seconds)
    if masked:
        pieces = struct((len(seconds) // 2, rank, seconds[0].shape[0]), f32)
        outs = [pieces, pieces]
    else:
        outs = [struct((rank, outer), f32)]
    return call(
        functools.partial(two_sided_kernel, len(lefts), len(firsts), len(seconds), masked),
        outs,
        (*lefts, *firsts, *seconds),
        (fill,),
        in_specs=[whole(x) for x in (*lefts, *firsts, *seconds)],
        out_specs=[whole(o) for o in outs],
        scratch=[
            pltpu.VMEM((2 * rank, inner), bf16),
            pltpu.VMEM((inner, total), bf16),
            pltpu.VMEM((outer, total), bf16),
        ],
        flops=4 * rank * (inner + outer) * total,
    )


def eliminate(grams):
    rank = grams[0].shape[0]
    group = 4
    wide = 2 * rank
    row = lax.broadcasted_iota(jnp.int32, (rank, wide), 0)
    column = lax.broadcasted_iota(jnp.int32, (rank, rank), 1)
    one = (lax.broadcasted_iota(jnp.int32, (rank, rank), 0) == column).astype(f32)
    state = [jnp.concatenate([g, one], axis=1) for g in grams]
    scale = [jnp.ones((rank, wide), f32) for _ in grams]
    for first in range(0, rank, group):
        columns = [
            [jnp.broadcast_to(m[:, first + k : first + k + 1], (rank, wide)) for k in range(group)]
            for m in state
        ]
        for k in range(group):
            j = first + k
            for t in range(len(grams)):
                pivot = columns[t][k][j : j + 1, :]
                factor = jnp.where(row > j, columns[t][k] * (1.0 / pivot), 0.0)
                state[t] = state[t] - factor * state[t][j : j + 1, :]
                for q in range(k + 1, group):
                    columns[t][q] = columns[t][q] - factor * columns[t][q][j : j + 1, :]
                scale[t] = jnp.where(row == j, lax.rsqrt(pivot), scale[t])
    return [(m * c)[:, rank:] for m, c in zip(state, scale)]


def factor_kernel(count, me_ref, gram_ref, down_ref, *refs):
    up_refs, outs = refs[:count], refs[count:]
    up = jnp.concatenate([r[...] for r in up_refs], axis=1)
    gram_up = dot(up, up, (1, 1), HIGHEST)
    inverses = eliminate([gram_up, gram_ref[...]])
    natural = jnp.concatenate(reorder([r[...] for r in up_refs], me_ref[0]), axis=1)
    for t, proj in enumerate((natural, down_ref[...])):
        outs[t][...] = inverses[t]
        head, tail = head_tail(dot(inverses[t], proj, precision=HIGHEST))
        outs[2 + t][...] = jnp.concatenate([head, head, tail], axis=0).T


def factor(proj_up, proj_down, gram_down, me):
    rank, units = proj_down.shape
    features = sum(p.shape[1] for p in proj_up)
    outs = [struct((rank, rank), f32)] * 2 + [struct((features, 3 * rank), bf16), struct((units, 3 * rank), bf16)]
    args = (gram_down, proj_down, *proj_up)
    return call(
        functools.partial(factor_kernel, len(proj_up)),
        outs,
        args,
        (me.reshape(1),),
        in_specs=[whole(a) for a in args],
        out_specs=[whole(o) for o in outs],
        flops=1 << 28,
    )


def outer_kernel(n_raw, me_ref, inv_ref, left_ref, *refs):
    raw_refs, (fresh_ref, approx_ref, right) = refs[:n_raw], refs[n_raw:]

    @pl.when(pl.program_id(0) == 0)
    def _():
        raw = jnp.concatenate(reorder([r[...] for r in raw_refs], me_ref[0]), axis=1)
        fresh = dot(inv_ref[...], raw, precision=HIGHEST)
        fresh_ref[...] = fresh
        head, tail = head_tail(fresh)
        right[...] = jnp.concatenate([head, tail, head], axis=0)

    approx_ref[...] = dot(left_ref[...], right[...])


def outer(inv, left, raws, me):
    rows, triple = left.shape
    columns = sum(r.shape[1] for r in raws)
    strip = rows // 2
    outs = [struct((triple // 3, columns), f32), struct((rows, columns), f32)]
    return call(
        functools.partial(outer_kernel, len(raws)),
        outs,
        (inv, left, *raws),
        (me.reshape(1),),
        grid=(rows // strip,),
        in_specs=[whole(inv), pl.BlockSpec((strip, triple), lambda i, *_: (i, 0))] + [whole(r) for r in raws],
        out_specs=[whole(outs[0]), pl.BlockSpec((strip, columns), lambda i, *_: (i, 0))],
        scratch=[pltpu.VMEM((triple, columns), bf16)],
        flops=2 * triple * rows * columns,
    )


def pack_kernel(index_ref, ok_ref, a_ref, b_ref, out_ref):
    piece = a_ref.shape[0]
    for s in range(out_ref.shape[0]):
        lanes = pl.ds(pl.multiple_of(index_ref[s] * BLOCK, BLOCK), BLOCK)
        total = a_ref[:, lanes].astype(f32) + b_ref[:, lanes].astype(f32)
        out_ref[s, :piece, :] = total.astype(bf16)
        out_ref[s, piece:, :] = jnp.full((FLAG, BLOCK), ok_ref[s].astype(f32)).astype(bf16)


def pack(a, b, index, ok):
    out = struct((index.shape[0], a.shape[0] + FLAG, BLOCK), bf16)
    return call(pack_kernel, out, (a, b), (index, ok), in_specs=[whole(a), whole(b)], out_specs=whole(out))


def unpack_kernel(in_ref, out_ref):
    piece = out_ref.shape[0]
    out_ref[...] = jnp.zeros_like(out_ref)
    used = [jnp.max(in_ref[s, piece:, :].astype(f32)).astype(jnp.int32) for s in range(in_ref.shape[0])]
    at = jnp.int32(0)
    for s, one in enumerate(used):

        @pl.when(one > 0)
        def _(s=s, at=at):
            lanes = pl.ds(pl.multiple_of(at * BLOCK, BLOCK), BLOCK)
            out_ref[:, lanes] = in_ref[s, :piece, :]

        at = at + one


def unpack(got, most):
    out = struct((got.shape[1] - FLAG, most * BLOCK), bf16)
    return call(unpack_kernel, out, (got,), in_specs=[whole(got)], out_specs=whole(out))


def earlier(labels):
    ids = jnp.arange(labels.shape[0], dtype=jnp.int32)
    same = (labels[:, None] == labels[None, :]) & (ids[None, :] < ids[:, None])
    return jnp.sum(same.astype(jnp.int32), axis=1)


def send_plan(ranks, ranks_dp):
    place = ranks * CAP + earlier(ranks)
    chosen = jnp.arange(ranks_dp * CAP, dtype=jnp.int32)[:, None] == place[None, :]
    ids = jnp.arange(ranks.shape[0], dtype=jnp.int32)
    index = jnp.sum(jnp.where(chosen, ids[None, :], 0), axis=1)
    return index.astype(jnp.int32), jnp.any(chosen, axis=1).astype(jnp.int32)


def split_rows(x):
    head = lax.reduce_precision(x, 8, 7)
    return jnp.concatenate([head.astype(bf16), (x - head).astype(bf16)], axis=0)


def local(patches, cotangent, encoder_rank, block_fill, w_up, w_down, q_up, q_down):
    ranks_dp = lax.axis_size("dp")
    count = lax.axis_size("mp")
    me = lax.axis_index("mp")
    blocks = encoder_rank.shape[0]

    xs = gather_xor(patches.T)
    cs = gather_xor(cotangent.T)
    up_t, down_t, down_x = prepare(w_up, w_down, me, count)
    qd = split_rows(jnp.concatenate(reorder(slices(q_down.T, count, 1), me), axis=1))
    qu = split_rows(q_up.T)

    hidden, slope, outs = forward(xs, up_t, down_t, block_fill)
    grad_pre, even, odd, proj_down = backward(cs, xs, slope, hidden, down_x, qu, qd, block_fill)

    have = {o: outs[o].astype(f32) for o in range(0, count, 2)}
    have = {o: (h + swap(outs[o | 1], "mp", 1).astype(f32)).astype(bf16) for o, h in have.items()}
    for bit in bits_of(count)[1:]:
        got = {o ^ bit: swap(have[o], "mp", bit) for o in have if o & bit}
        if len(got) == 1:
            break
        have = {o: (have[o].astype(f32) + got[o].astype(f32)).astype(bf16) for o in got}
    sent = pack(have[0], got[0], *send_plan(encoder_rank, ranks_dp))
    received = lax.all_to_all(sent, "dp", split_axis=0, concat_axis=0, tiled=True)
    encoded = unpack(received, blocks + EXTRA)

    proj_down = sum_over(proj_down, "dp", bf16)
    proj_up = sum_over(reduce_mp(even, odd), "dp", f32)
    proj_up = spread_mp(proj_up)

    even, odd = two_sided([proj_down], [hidden], cs, block_fill, True)
    (raw_up,) = two_sided(proj_up, xs, [grad_pre], block_fill, False)

    gram_down = sum_over(dot(proj_down, proj_down, (1, 1), HIGHEST), "mp", f32)
    inv_up, inv_down, left_up, left_down = factor(proj_up, proj_down, gram_down, me)

    raw_down = sum_over(reduce_mp(even, odd), "dp", f32)
    raw_up = sum_over(raw_up, "dp", bf16)
    raw_down = spread_mp(raw_down)
    fresh_up, approx_up = outer(inv_up, left_up, [raw_up], me)
    fresh_down, approx_down = outer(inv_down, left_down, raw_down, me)
    return (encoded.T, approx_up, approx_down, fresh_up.T, fresh_down.T)


def solution(mesh):
    placed = (
        P("dp", "mp"),
        P("dp", "mp"),
        P("dp"),
        P("dp"),
        P(None, "mp"),
        P("mp", None),
        P("mp", None),
        P(),
    )
    return jax.shard_map(
        local,
        mesh=mesh,
        in_specs=placed,
        out_specs=(P("dp", "mp"), P(None, "mp"), P("mp", None), P("mp", None), P()),
        check_vma=False,
    )
```
